512 devices in a mesh: leaf: 64 (over y, x, core), probe: 8 (over z).
Axes of the slice: x: 4, y: 8, z: 8, core: 2. Of those that a mesh axis runs over, the one named last changes fastest.
Arguments:
- coef_fine: bfloat16 [64, 262144], P('probe', 'leaf'), may hold values from -0.59765625 to 0.59765625
- points_fine: float32 [3, 262144], P(None, 'leaf'), may hold values from -1 to 1
- points_coarse: float32 [3, 131072], P(None, 'leaf'), may hold values from -1 to 1
- transfer: bfloat16 [64, 262144], P(None, 'leaf'), may hold values from -0.5 to 0.5
- send_fine: int32 [64, 64, 16], P('leaf'), may hold values from 0 to 63, as said below
- slots_fine: int32 [4096, 64], P('leaf'), may hold values from 0 to 1087, as said below
- counts_fine: int32 [4096], P('leaf'), may hold values from 1 to 64, as said below
- send_coarse: int32 [64, 64, 8], P('leaf'), may hold values from 0 to 31, as said below
- slots_coarse: int32 [2048, 64], P('leaf'), may hold values from 0 to 543, as said below
- counts_coarse: int32 [2048], P('leaf'), may hold values from 1 to 64, as said below
Outputs:
- far_field: float32 [64, 262144], P('probe', 'leaf')
- probe_gram: float32 [64, 64], P('probe')
The draws below stay inside these ranges and needn't reach their ends.
Inputs may be any that keep to these rules, and one draw needn't show every extreme that they name: `send_fine`: entry [e, d, i] is the local index of a cluster of device e that device e sends to device d; every device sends exactly 16 distinct clusters to every device, itself included. `slots_fine`: A slot value v below 64 names the owning device's own cluster v; a value of 64 or more names entry [(v - 64) // 16, owner, (v - 64) % 16] of send_fine. Only the first counts_fine[c] slots of cluster c are live; every device has a cluster with all 64 slots live. `send_coarse`: entry [e, d, i] is the local index of a cluster of device e that device e sends to device d; every device sends exactly 8 distinct clusters to every device, itself included. `slots_coarse`: A slot value v below 32 names the owning device's own cluster v; a value of 32 or more names entry [(v - 32) // 8, owner, (v - 32) % 8] of send_coarse. Only the first counts_coarse[q] slots of cluster q are live; every device has a cluster with all 64 slots live.
All inputs are finite; a program needn't handle non-finite values.
Results may differ from the reference program's by a relative error of at most 0.0036.
Values may be sent and summed in bfloat16 or wider, within the bound.
A program may use at most 64 MiB of HBM per device.

```python
import math
import jax
import jax.numpy as jnp
from jax import lax

K = 64
P_SIZE = 64
PAIRS = 64
CF = 64
CC = 32
CAP_F = 16
CAP_C = 8
OWNERS = 64
NF = 4096
NC = 2048


def pick_lists(key, clusters, capacity):
    member_keys = jax.random.split(key, OWNERS * OWNERS)
    chosen_rows = jax.vmap(lambda member: jax.random.permutation(member, clusters)[:capacity])(member_keys)
    return chosen_rows.reshape(OWNERS, OWNERS, capacity).astype(jnp.int32)


def pick_slots(key, clusters, capacity):
    first_key, second_key, third_key = jax.random.split(key, 3)
    total = OWNERS * clusters
    chooser = jax.random.randint(first_key, (total, PAIRS), 0, 4)
    own_slot = jax.random.randint(second_key, (total, PAIRS), 0, clusters)
    remote_slot = clusters + jax.random.randint(third_key, (total, PAIRS), 0, OWNERS * capacity)
    return jnp.where(chooser == 0, own_slot, remote_slot).astype(jnp.int32)


def pick_counts(key, clusters):
    first_key, second_key, third_key = jax.random.split(key, 3)
    stride = max(1, PAIRS // 8)
    lowest = jax.random.randint(first_key, (OWNERS,), 1, 6) * stride
    drawn = jax.random.randint(second_key, (OWNERS, clusters), lowest[:, None], PAIRS + 1)
    position = jax.random.randint(third_key, (OWNERS,), 0, clusters)
    column = jnp.arange(clusters, dtype=jnp.int32)[None, :]
    filled = jnp.where(column == position[:, None], PAIRS, drawn)
    return filled.reshape(OWNERS * clusters).astype(jnp.int32)


def draw_send_fine(key, part):
    return pick_lists(jax.random.fold_in(key, 11), CF, CAP_F)


def draw_slots_fine(key, part):
    return pick_slots(jax.random.fold_in(key, 12), CF, CAP_F)


def draw_counts_fine(key, part):
    return pick_counts(jax.random.fold_in(key, 13), CF)


def draw_send_coarse(key, part):
    return pick_lists(jax.random.fold_in(key, 21), CC, CAP_C)


def draw_slots_coarse(key, part):
    return pick_slots(jax.random.fold_in(key, 22), CC, CAP_C)


def draw_counts_coarse(key, part):
    return pick_counts(jax.random.fold_in(key, 23), CC)


def block_scale(rng, shape, shards, low, largest):
    factor_of = 1.0
    for dim, parts in shards:
        draws = jax.random.uniform(jax.random.fold_in(jax.random.fold_in(rng, 6), dim), (parts,), jnp.float32, low / len(shards), largest / len(shards))
        factor_of = factor_of * jnp.repeat(jnp.exp(draws), shape[dim] // parts).reshape((-1,) + (1,) * (len(shape) - 1 - dim))
    return factor_of


def centred(stream_key, extent, deviation, most, cuts=(), kind=jnp.bfloat16):
    factor_of = block_scale(stream_key, extent, cuts, -0.22, 0.18) if cuts else 1.0
    values = jax.random.normal(stream_key, extent, jnp.float32) * deviation * factor_of
    return jnp.minimum(jnp.maximum(values, -most), most).astype(kind)


def setup_inputs(seed: int = 0) -> dict:
    seeds = jax.random.split(jax.random.key(seed), 11)
    return {
        "coef_fine": centred(seeds[0], (P_SIZE, NF * K), 0.1, 0.59765625, ((0, 8), (1, 64))),
        "points_fine": jnp.clip(jax.random.uniform(seeds[1], (3, NF * K), jnp.float32, -1.0, 1.0) * block_scale(seeds[1], (3, NF * K), ((1, 64),), -0.4, 0.0), -1.0, 1.0),
        "points_coarse": jnp.clip(jax.random.uniform(seeds[2], (3, NC * K), jnp.float32, -1.0, 1.0) * block_scale(seeds[2], (3, NC * K), ((1, 64),), -0.4, 0.0), -1.0, 1.0),
        "transfer": centred(seeds[3], (K, NF * K), (2 * K) ** -0.5, 0.5, ((1, 64),)),
        "send_fine": draw_send_fine(jax.random.fold_in(seeds[10], 71), 0),
        "slots_fine": draw_slots_fine(jax.random.fold_in(seeds[10], 71), 0),
        "counts_fine": draw_counts_fine(jax.random.fold_in(seeds[10], 71), 0),
        "send_coarse": draw_send_coarse(jax.random.fold_in(seeds[10], 71), 0),
        "slots_coarse": draw_slots_coarse(jax.random.fold_in(seeds[10], 71), 0),
        "counts_coarse": draw_counts_coarse(jax.random.fold_in(seeds[10], 71), 0),
    }


kernel_rate = 1.5

def kernel_block(target, source):
    squared = jnp.zeros((source.shape[0], target.shape[1], source.shape[2]), jnp.float32)
    for coord in range(3):
        coord_delta = target[coord][None, :, None] - source[:, coord][:, None, :]
        squared = squared + coord_delta * coord_delta
    return jnp.exp(-kernel_rate * squared)

def partner_ids(slot_row, owner_index, per_device, capacity, send_lists):
    offset = slot_row - per_device
    source = jnp.clip(offset // capacity, 0, OWNERS - 1).astype(jnp.int32)
    within = jnp.where(offset >= 0, offset % capacity, 0).astype(jnp.int32)
    remote = source * per_device + send_lists[source, owner_index, within]
    return jnp.where(slot_row < per_device, owner_index * per_device + slot_row, remote).astype(jnp.int32)

def level_sweep(coef_rows, point_rows, send_lists, slot_table, count_table, per_device, capacity):

    def one_cluster(cluster_item):
        target, slot_row, pair_count = cluster_item
        owner_index = (target // per_device).astype(jnp.int32)
        partner = partner_ids(slot_row, owner_index, per_device, capacity, send_lists)
        kernel_tile = kernel_block(point_rows[target], point_rows[partner])
        live_mask = jnp.arange(PAIRS, dtype=jnp.int32) < pair_count
        weights = jnp.where(live_mask[:, None, None], kernel_tile, 0.0).astype(jnp.bfloat16)
        return jnp.einsum('mkj,mpj->pk', weights.astype(jnp.float32), coef_rows[partner].astype(jnp.float32))
    return lax.map(one_cluster, (jnp.arange(coef_rows.shape[0], dtype=jnp.int32), slot_table, count_table))

def reference(coef_fine, points_fine, points_coarse, transfer, send_fine, slots_fine, counts_fine, send_coarse, slots_coarse, counts_coarse):
    coef_rows = coef_fine.reshape(P_SIZE, NF, K).transpose(1, 0, 2)
    fine_points = points_fine.reshape(3, NF, K).transpose(1, 0, 2)
    coarse_points = points_coarse.reshape(3, NC, K).transpose(1, 0, 2)
    matrices = transfer.reshape(K, NC, 2, K).astype(jnp.float32)
    children = coef_rows.reshape(NC, 2, P_SIZE, K).astype(jnp.float32)
    coarse_coef = jnp.einsum('qcpk,kqcj->qpj', children, matrices).astype(jnp.bfloat16)
    fine_far = level_sweep(coef_rows, fine_points, send_fine, slots_fine, counts_fine, CF, CAP_F)
    coarse_far = level_sweep(coarse_coef, coarse_points, send_coarse, slots_coarse, counts_coarse, CC, CAP_C).astype(jnp.bfloat16)
    downward = jnp.einsum('qpj,kqcj->qcpk', coarse_far.astype(jnp.float32), matrices).reshape(NF, P_SIZE, K)
    combined = fine_far + downward
    far_field = combined.transpose(1, 0, 2).reshape(P_SIZE, NF * K)
    probe_gram = jnp.dot(coef_fine.astype(jnp.float32), far_field.T, precision=lax.Precision.HIGHEST) * (1.0 / math.sqrt(NF * K))
    return (far_field, probe_gram)
```

```python
import functools
import math

import jax
import jax.numpy as jnp
from jax import lax
from jax.experimental import pallas as pl
from jax.experimental.pallas import tpu as pltpu
from jax.sharding import PartitionSpec as P

kernel_rate = 1.5
LOG2E = 1.4426950408889634
RANK = 64
NX, NY, NZ = 4, 8, 8
CHIPS = NX * NY
FINE, COARSE, PAIRS = 64, 32, 64
FT, CT = FINE // 2, COARSE // 2
TILES = FT + CT + 1
LIST_TILE = FT + CT
ROWS = 2 * CHIPS * TILES
ZERO = ROWS
SPAN = ROWS + 8
MESH = pl.DeviceIdType.MESH
F32, BF16 = jnp.float32, jnp.bfloat16
NT = (((1,), (1,)), ((), ()))
VMEM_LIMIT = 60 * 1024 * 1024


def features(points):
    high = points.astype(BF16).astype(F32)
    low = (points - high).astype(BF16).astype(F32)
    squares = points[0:1] * points[0:1] + points[1:2] * points[1:2] + points[2:3] * points[2:3]
    bias = squares * (-kernel_rate * LOG2E)
    bias_high = bias.astype(BF16).astype(F32)
    bias_low = (bias - bias_high).astype(BF16).astype(F32)
    scaled = points * (2.0 * kernel_rate * LOG2E)
    scaled_high = scaled.astype(BF16).astype(F32)
    scaled_low = (scaled - scaled_high).astype(BF16).astype(F32)
    ones = jnp.ones((2, points.shape[1]), F32)
    nothing = jnp.zeros((8, points.shape[1]), F32)
    source = jnp.concatenate([high, low, bias_high, bias_low], axis=0)
    target = jnp.concatenate(
        [
            scaled_high,
            scaled_high,
            ones,
            nothing,
            scaled_low,
            scaled_low,
            nothing[0:2],
            nothing,
        ],
        axis=0,
    )
    return source, target, jnp.exp(squares * -kernel_rate)


def prep_kernel(coef, fine_pts, coarse_pts, transfer, lists, payload, target_out, scale_out):
    source, target, scale = features(fine_pts[...])
    rows = jnp.concatenate([source, coef[...].astype(F32)], axis=0).astype(BF16)
    target = target.astype(BF16)
    for t in range(FT):
        cut = slice(t * 128, t * 128 + 128)
        payload[t] = rows[:, cut]
        target_out[t] = target[:, cut]
    scale_out[:, 0 : FT * 128] = jnp.broadcast_to(scale, (8, FT * 128))
    source, target, scale = features(coarse_pts[...])
    target = target.astype(BF16)
    for t in range(CT):
        halves = []
        for q in (2 * t, 2 * t + 1):
            mats = transfer[:, q * 128 : q * 128 + 128]
            left = jnp.dot(
                coef[:, q * 128 : q * 128 + 64], mats, preferred_element_type=F32
            )
            right = jnp.dot(
                coef[:, q * 128 + 64 : q * 128 + 128], mats, preferred_element_type=F32
            )
            halves.append(left[:, 0:64] + right[:, 64:128])
        cut = slice(t * 128, t * 128 + 128)
        rows = jnp.concatenate([source[:, cut], jnp.concatenate(halves, axis=1)], axis=0)
        payload[FT + t] = rows.astype(BF16)
        target_out[FT + t] = target[:, cut]
    scale_out[:, FT * 128 :] = jnp.broadcast_to(scale, (8, CT * 128))
    payload[LIST_TILE] = lists[...]


def prep(coef, fine_pts, coarse_pts, transfer, lists):
    return pl.pallas_call(
        prep_kernel,
        out_shape=(
            jax.ShapeDtypeStruct((TILES, 16, 128), BF16),
            jax.ShapeDtypeStruct((FT + CT, 32, 128), BF16),
            jax.ShapeDtypeStruct((8, (FT + CT) * 128), F32),
        ),
        compiler_params=pltpu.CompilerParams(vmem_limit_bytes=VMEM_LIMIT),
        name="prep",
    )(coef, fine_pts, coarse_pts, transfer, lists)


FLOWS = (
    (True, 1, 0, 10),
    (True, -1, 10, 20),
    (False, 1, 20, 35),
    (False, -1, 35, 49),
)


def spread_kernel(
    payload, coef, table, probes, link_recv, link_send, chip_recv, chip_send, z_recv, z_send, own_sem
):
    leaf = lax.axis_index("leaf")
    z = lax.axis_index("probe")
    core = lax.rem(leaf, 2)
    chip = leaf // 2
    x = lax.rem(chip, NX)
    y = chip // NX

    def chip_at(xs, ys):
        return lax.rem(y + ys + NY, NY) * NX + lax.rem(x + xs + NX, NX)

    def leaf_at(xs, ys):
        return chip_at(xs, ys) * 2 + core

    twin = chip * 2 + (1 - core)
    barrier = pltpu.get_barrier_semaphore()
    peers = [leaf_at(1, 0), leaf_at(-1, 0), leaf_at(0, 1), leaf_at(0, -1), twin]
    for peer in peers:
        pl.semaphore_signal(barrier, 1, device_id={"leaf": peer}, device_id_type=MESH)
    for s in range(1, NZ):
        pl.semaphore_signal(
            barrier, 1, device_id={"probe": lax.rem(z + s, NZ)}, device_id_type=MESH
        )
    pl.semaphore_wait(barrier, len(peers) + NZ - 1)

    own = pltpu.make_async_copy(payload, table.at[core, chip], own_sem.at[0])
    own.start()
    own_coef = pltpu.make_async_copy(coef, probes.at[z], own_sem.at[1])
    own_coef.start()

    def piece(f, i, j):
        _, sign, low, high = FLOWS[f]
        return table.at[core, chip_at(-sign * i, -sign * j), low:high]

    def source(f, i, j):
        _, _, low, high = FLOWS[f]
        return payload.at[low:high] if i == 0 and j == 0 else piece(f, i, j)

    def push(f, i, j, along_x):
        _, sign, _, _ = FLOWS[f]
        peer = leaf_at(sign, 0) if along_x else leaf_at(0, sign)
        slot = (i + 1, j) if along_x else (i, j + 1)
        pltpu.make_async_remote_copy(
            source(f, i, j),
            piece(f, i, j),
            link_send,
            link_recv.at[f, slot[0], slot[1]],
            device_id={"leaf": peer},
            device_id_type=MESH,
        ).start()

    def share(f, i, j):
        pltpu.make_async_remote_copy(
            source(f, i, j),
            piece(f, i, j),
            chip_send,
            chip_recv,
            device_id={"leaf": twin},
            device_id_type=MESH,
        ).start()

    for t in range(NX + NY - 1):
        for i in range(NX):
            j = t - i
            if j < 0 or j >= NY:
                continue
            for f in range(4):
                x_first = FLOWS[f][0]
                if t > 0:
                    part = piece(f, i, j)
                    pltpu.make_async_copy(part, part, link_recv.at[f, i, j]).wait()
                if x_first:
                    if j == 0 and i < NX - 1:
                        push(f, i, j, True)
                    if j < NY - 1:
                        push(f, i, j, False)
                else:
                    if i == 0 and j < NY - 1:
                        push(f, i, j, False)
                    if i < NX - 1:
                        push(f, i, j, True)
                share(f, i, j)
        if t == 0:
            for s in range(1, NZ):
                pltpu.make_async_remote_copy(
                    coef,
                    probes.at[z],
                    z_send,
                    z_recv,
                    device_id={"probe": lax.rem(z + s, NZ)},
                    device_id_type=MESH,
                ).start()

    own.wait()
    own_coef.wait()
    half = table.at[1 - core]
    pltpu.make_async_copy(half, half, chip_recv).wait()
    half = table.at[core]
    pltpu.make_async_copy(half, half, chip_send).wait()
    sent = table.at[core, 0 : CHIPS - 1]
    pltpu.make_async_copy(sent, sent, link_send).wait()
    others = probes.at[0 : NZ - 1]
    pltpu.make_async_copy(others, others, z_recv).wait()
    pltpu.make_async_copy(others, others, z_send).wait()


def spread(payload, coef):
    dma = pltpu.SemaphoreType.DMA
    return pl.pallas_call(
        spread_kernel,
        out_shape=(
            jax.ShapeDtypeStruct((2, CHIPS, TILES, 16, 128), BF16),
            jax.ShapeDtypeStruct((NZ,) + coef.shape, BF16),
        ),
        in_specs=[pl.BlockSpec(memory_space=pl.ANY)] * 2,
        out_specs=[pl.BlockSpec(memory_space=pl.ANY)] * 2,
        scratch_shapes=[
            dma((4, NX, NY)),
            dma(()),
            dma(()),
            dma(()),
            dma(()),
            dma(()),
            dma((2,)),
        ],
        compiler_params=pltpu.CompilerParams(collective_id=0, has_side_effects=True),
        name="spread",
    )(payload, coef)


CHUNKS = 8
PER = ROWS // CHUNKS


def sweep_kernel(
    fine_slots,
    coarse_slots,
    fine_rows,
    coarse_rows,
    table,
    target_feats,
    scale,
    probes,
    transfer,
    far,
    partial,
    tiles,
    sems,
):
    z = lax.axis_index("probe")

    def fetch(n):
        return pltpu.make_async_copy(
            table.at[pl.ds(n * PER, PER)], tiles.at[pl.ds(n * PER, PER)], sems.at[n]
        )

    for n in range(CHUNKS):
        fetch(n).start()
    tiles[ZERO] = jnp.zeros((16, 128), BF16)
    tiles[SPAN + ZERO] = jnp.zeros((16, 128), BF16)
    for n in range(CHUNKS):
        fetch(n).wait()

        def swap(i, carry):
            for u in range(8):
                at = n * PER + i * 8 + u
                block = tiles[at]
                tiles[SPAN + at] = jnp.concatenate([block[:, 64:], block[:, :64]], axis=1)
            return carry

        lax.fori_loop(0, PER // 8, swap, 0)

    left_half = lax.broadcasted_iota(jnp.int32, (16, 128), 1) < 64

    def gather_pair(slots, rows, s, m):
        first = tiles[rows[0, slots[s, m]]]
        second = tiles[rows[1, slots[s, m + 1]]]
        return jnp.where(left_half, first, second)

    def one_target(slots, rows, s, feats):
        total = jnp.zeros((16, RANK), F32)
        for m in range(0, PAIRS, 4):
            both = jnp.concatenate(
                [gather_pair(slots, rows, s, m), gather_pair(slots, rows, s, m + 2)], axis=1
            )
            exponent = lax.dot_general(
                feats,
                jnp.concatenate([both, both], axis=0),
                (((1,), (0,)), ((), ())),
                preferred_element_type=F32,
            )
            weights = jnp.exp2(exponent).astype(BF16)
            total = total + lax.dot_general(both, weights, NT, preferred_element_type=F32)
        return total[8:16]

    def feats_of(t):
        return target_feats[t].astype(F32).T.astype(BF16)

    def coarse_feats(q):
        return feats_of(FT + q // 2)

    def step(q2, carry):
        coarse_pair = feats_of(FT + q2)
        for h in range(2):
            q = q2 * 2 + h
            fine_pair = feats_of(q)
            up = one_target(coarse_slots, coarse_rows, q, coarse_pair[h * 64 : h * 64 + 64])
            low = one_target(fine_slots, fine_rows, 2 * q, fine_pair[0:64])
            high = one_target(fine_slots, fine_rows, 2 * q + 1, fine_pair[64:128])
            at = pl.ds(pl.multiple_of((FT + q2) * 128, 128), 128)
            up = up * scale[:, at][:, h * 64 : h * 64 + 64]
            mats = transfer[:, pl.ds(pl.multiple_of(q * 128, 128), 128)]
            empty = jnp.zeros((8, RANK), F32)
            spread_up = jnp.concatenate(
                [
                    jnp.concatenate([up, empty], axis=1),
                    jnp.concatenate([empty, up], axis=1),
                ],
                axis=0,
            ).astype(BF16)
            down = lax.dot_general(spread_up, mats, NT, preferred_element_type=F32)
            cut = pl.ds(pl.multiple_of(q * 128, 128), 128)
            near = jnp.concatenate([low, high], axis=1) * scale[:, cut]
            far[:, cut] = near + jnp.concatenate([down[0:8], down[8:16]], axis=1)
        return carry

    lax.fori_loop(0, CT, step, 0)

    whole = far[...]
    first = whole.astype(BF16)
    rest = whole - first.astype(F32)
    second = rest.astype(BF16)
    third = (rest - second.astype(F32)).astype(BF16)
    coefs = probes[...].reshape(NZ * 8, FINE * RANK)
    gram = (
        lax.dot_general(coefs, first, NT, preferred_element_type=F32)
        + lax.dot_general(coefs, second, NT, preferred_element_type=F32)
        + lax.dot_general(coefs, third, NT, preferred_element_type=F32)
    )
    wide = jnp.concatenate([gram, jnp.zeros((NZ * 8, 120), F32)], axis=1)
    partial[...] = pltpu.roll(wide, z * 8, 1)


def sweep(fine_slots, coarse_slots, fine_rows, coarse_rows, table, feats, scale, probes, transfer):
    vm = pl.BlockSpec(memory_space=pltpu.VMEM)
    sm = pl.BlockSpec(memory_space=pltpu.SMEM)
    return pl.pallas_call(
        sweep_kernel,
        out_shape=(
            jax.ShapeDtypeStruct((8, FINE * RANK), F32),
            jax.ShapeDtypeStruct((NZ * 8, 128), F32),
        ),
        in_specs=[sm, sm, sm, sm, pl.BlockSpec(memory_space=pl.ANY), vm, vm, vm, vm],
        out_specs=[vm, vm],
        scratch_shapes=[
            pltpu.VMEM((2 * SPAN, 16, 128), BF16),
            pltpu.SemaphoreType.DMA((CHUNKS,)),
        ],
        compiler_params=pltpu.CompilerParams(vmem_limit_bytes=VMEM_LIMIT),
        name="sweep",
    )(fine_slots, coarse_slots, fine_rows, coarse_rows, table, feats, scale, probes, transfer)


def reduce_kernel(gram_scale, partial, out, at_z, at_x, at_y, work, recv, send):
    leaf = lax.axis_index("leaf")
    z = lax.axis_index("probe")
    inner = lax.rem(leaf, 2 * NX)
    y = leaf // (2 * NX)

    def z_peer(s):
        return {"probe": lax.rem(z + s, NZ)}

    def x_peer(s):
        return {"leaf": y * (2 * NX) + lax.rem(inner + s, 2 * NX)}

    def y_peer(s):
        return {"leaf": lax.rem(y + s, NY) * (2 * NX) + inner}

    barrier = pltpu.get_barrier_semaphore()
    for peer in (z_peer, x_peer, y_peer):
        for s in range(1, 8):
            pl.semaphore_signal(barrier, 1, device_id=peer(s), device_id_type=MESH)
    pl.semaphore_wait(barrier, 21)

    def exchange(stage, peer, me, source, buffer):
        for s in range(1, 8):
            pltpu.make_async_remote_copy(
                source(s),
                buffer.at[me],
                send.at[stage],
                recv.at[stage],
                device_id=peer(s),
                device_id_type=MESH,
            ).start()
        buffer[me] = source(0)[...]
        got = buffer.at[0:7]
        pltpu.make_async_copy(got, got, recv.at[stage]).wait()
        total = buffer[0]
        for n in range(1, 8):
            total = total + buffer[n]
        pltpu.make_async_copy(got, got, send.at[stage]).wait()
        return total

    work[0] = exchange(0, z_peer, z, lambda s: partial.at[lax.rem(z + s, NZ)], at_z)
    work[1] = exchange(1, x_peer, inner, lambda s: work.at[0], at_x)
    out[...] = exchange(2, y_peer, y, lambda s: work.at[1], at_y) * gram_scale


def reduce_gram(partial, gram_scale):
    vm = pl.BlockSpec(memory_space=pltpu.VMEM)
    return pl.pallas_call(
        functools.partial(reduce_kernel, gram_scale),
        out_shape=jax.ShapeDtypeStruct((8, 128), F32),
        in_specs=[vm],
        out_specs=vm,
        scratch_shapes=[
            pltpu.VMEM((8, 8, 128), F32),
            pltpu.VMEM((8, 8, 128), F32),
            pltpu.VMEM((8, 8, 128), F32),
            pltpu.VMEM((2, 8, 128), F32),
            pltpu.SemaphoreType.DMA((3,)),
            pltpu.SemaphoreType.DMA((3,)),
        ],
        compiler_params=pltpu.CompilerParams(collective_id=1, has_side_effects=True),
        name="reduce_gram",
    )(partial)


def row_tables(lists, leaf, clusters, offset):
    capacity = lists.shape[1]
    owner = jnp.arange(2 * CHIPS, dtype=jnp.int32)
    base = ((owner % 2) * CHIPS + owner // 2) * TILES + offset
    mine = (lax.rem(leaf, 2) * CHIPS + leaf // 2) * TILES + offset
    local = jnp.arange(clusters, dtype=jnp.int32)
    tile = jnp.concatenate(
        [mine + local // 2, (base[:, None] + lists // 2).reshape(2 * CHIPS * capacity)]
    )
    odd = jnp.concatenate([local % 2, (lists % 2).reshape(2 * CHIPS * capacity)])
    rows = jnp.stack([tile + odd * SPAN, tile + (1 - odd) * SPAN])
    return jnp.pad(rows, ((0, 0), (0, 1)), constant_values=ZERO)


def masked(slots, counts):
    live = lax.broadcasted_iota(jnp.int32, slots.shape, 1) < counts[:, None]
    return live


def shards(
    coef_fine,
    points_fine,
    points_coarse,
    transfer,
    send_fine,
    slots_fine,
    counts_fine,
    send_coarse,
    slots_coarse,
    counts_coarse,
):
    leaf = lax.axis_index("leaf")
    cap_fine, cap_coarse = send_fine.shape[2], send_coarse.shape[2]
    lists = jnp.concatenate(
        [send_fine[0], send_coarse[0], jnp.zeros((64, 32 - cap_fine - cap_coarse), jnp.int32)],
        axis=1,
    )
    lists = lists.astype(BF16).reshape(16, 128)
    payload, feats, scale = prep(coef_fine, points_fine, points_coarse, transfer, lists)
    table, probes = spread(payload, coef_fine)
    got = table[:, :, LIST_TILE].transpose(1, 0, 2, 3).reshape(2 * CHIPS, 64, 32)
    got = lax.dynamic_index_in_dim(got, leaf, 1, keepdims=False).astype(jnp.int32)
    fine_rows = row_tables(got[:, 0:cap_fine], leaf, FINE, 0)
    coarse_rows = row_tables(got[:, cap_fine : cap_fine + cap_coarse], leaf, COARSE, FT)
    fine_slots = jnp.where(
        masked(slots_fine, counts_fine), slots_fine, FINE + 2 * CHIPS * cap_fine
    )
    coarse_slots = jnp.where(
        masked(slots_coarse, counts_coarse), slots_coarse, COARSE + 2 * CHIPS * cap_coarse
    )
    far, partial = sweep(
        fine_slots,
        coarse_slots,
        fine_rows,
        coarse_rows,
        table.reshape(ROWS, 16, 128),
        feats,
        scale,
        probes,
        transfer,
    )
    gram_scale = 1.0 / math.sqrt(2 * CHIPS * FINE * RANK)
    gram = reduce_gram(partial.reshape(NZ, 8, 128), gram_scale)
    return (far, gram[:, 0 : NZ * 8])


def solution(mesh):
    return jax.shard_map(
        shards,
        mesh=mesh,
        in_specs=(
            P("probe", "leaf"),
            P(None, "leaf"),
            P(None, "leaf"),
            P(None, "leaf"),
            P("leaf", None, None),
            P("leaf", None),
            P("leaf"),
            P("leaf", None, None),
            P("leaf", None),
            P("leaf"),
        ),
        out_specs=(P("probe", "leaf"), P("probe", None)),
        check_vma=False,
    )
```

```python
import functools
import math

import jax
import jax.numpy as jnp
from jax import lax
from jax.experimental import pallas as pl
from jax.experimental.pallas import tpu as pltpu
from jax.sharding import PartitionSpec as P

kernel_rate = 1.5
LOG2E = 1.4426950408889634
RANK = 64
NX, NY, NZ = 4, 8, 8
CHIPS = NX * NY
FINE, COARSE, PAIRS = 64, 32, 64
FT, CT = FINE // 2, COARSE // 2
HALF = FT + CT
TILES = HALF + 2
ROWS = 2 * CHIPS * TILES
SPAN = ROWS + 8
MESH = pl.DeviceIdType.MESH
F32, BF16 = jnp.float32, jnp.bfloat16
BATCH, LAG = 1, 12
UNROLL = 2
NT = (((1,), (1,)), ((), ()))
TABLE_SPACE = pltpu.VMEM
SPREAD_LIMIT = 20 * 1024 * 1024
SWEEP_LIMIT = 24 * 1024 * 1024


def features(points):
    high = points.astype(BF16).astype(F32)
    low = (points - high).astype(BF16).astype(F32)
    squares = points[0:1] * points[0:1] + points[1:2] * points[1:2] + points[2:3] * points[2:3]
    bias = squares * (-kernel_rate * LOG2E)
    bias_high = bias.astype(BF16).astype(F32)
    bias_low = (bias - bias_high).astype(BF16).astype(F32)
    scaled = points * (2.0 * kernel_rate * LOG2E)
    scaled_high = scaled.astype(BF16).astype(F32)
    scaled_low = (scaled - scaled_high).astype(BF16).astype(F32)
    ones = jnp.ones((2, points.shape[1]), F32)
    nothing = jnp.zeros((8, points.shape[1]), F32)
    source = jnp.concatenate([high, low, bias_high, bias_low], axis=0)
    target = jnp.concatenate(
        [
            scaled_high,
            scaled_high,
            ones,
            nothing,
            scaled_low,
            scaled_low,
            nothing[0:2],
            nothing,
            bias,
            nothing[0:7],
        ],
        axis=0,
    )
    return source, target


def prep_kernel(coef, fine_pts, coarse_pts, transfer, fine_list, coarse_list, payload, target_out):
    source, target = features(fine_pts[...])
    for t in range(FT):
        cut = slice(t * 128, t * 128 + 128)
        payload[t] = jnp.concatenate([source[:, cut], coef[:, cut].astype(F32)], axis=0).astype(BF16)
        target_out[t] = target[:, cut]
    source, target = features(coarse_pts[...])
    for t in range(CT):
        halves = []
        for q in (2 * t, 2 * t + 1):
            mats = transfer[:, q * 128 : q * 128 + 128]
            left = jnp.dot(
                coef[:, q * 128 : q * 128 + 64], mats, preferred_element_type=F32
            )
            right = jnp.dot(
                coef[:, q * 128 + 64 : q * 128 + 128], mats, preferred_element_type=F32
            )
            halves.append(left[:, 0:64] + right[:, 64:128])
        cut = slice(t * 128, t * 128 + 128)
        rows = jnp.concatenate([source[:, cut], jnp.concatenate(halves, axis=1)], axis=0)
        payload[FT + t] = rows.astype(BF16)
        target_out[FT + t] = target[:, cut]
    entries = [fine_list[...].astype(F32), coarse_list[...].astype(F32), jnp.zeros((8, 64), F32)]
    for n in range(2):
        part = entries[0] if n == 0 else jnp.concatenate(entries[1:], axis=0)
        payload[HALF + n] = jnp.concatenate([part, jnp.zeros((16, 64), F32)], axis=1).astype(BF16)


def prep(coef, fine_pts, coarse_pts, transfer, fine_list, coarse_list):
    return pl.pallas_call(
        prep_kernel,
        out_shape=(
            jax.ShapeDtypeStruct((TILES, 16, 128), BF16),
            jax.ShapeDtypeStruct((HALF, 40, 128), F32),
        ),
        compiler_params=pltpu.CompilerParams(vmem_limit_bytes=8 * 1024 * 1024),
        name="prep",
    )(coef, fine_pts, coarse_pts, transfer, fine_list, coarse_list)


FLOWS = (
    (True, 1, 0, 10),
    (True, -1, 10, 20),
    (False, 1, 20, 35),
    (False, -1, 35, 50),
)


def spread_kernel(
    payload, coef, table, probes, zeros, link_recv, link_send, chip_recv, chip_send, z_recv, z_send, own_sem
):
    leaf = lax.axis_index("leaf")
    z = lax.axis_index("probe")
    core = lax.rem(leaf, 2)
    chip = leaf // 2
    x = lax.rem(chip, NX)
    y = chip // NX

    def chip_at(xs, ys):
        return lax.rem(y + ys + NY, NY) * NX + lax.rem(x + xs + NX, NX)

    def leaf_at(xs, ys):
        return chip_at(xs, ys) * 2 + core

    twin = chip * 2 + (1 - core)
    barrier = pltpu.get_barrier_semaphore()
    peers = [leaf_at(1, 0), leaf_at(-1, 0), leaf_at(0, 1), leaf_at(0, -1), twin]
    for peer in peers:
        pl.semaphore_signal(barrier, 1, device_id={"leaf": peer}, device_id_type=MESH)
    for s in range(1, NZ):
        pl.semaphore_signal(
            barrier, 1, device_id={"probe": lax.rem(z + s, NZ)}, device_id_type=MESH
        )
    pl.semaphore_wait(barrier, len(peers) + NZ - 1)

    def rows_of(which_chip, low, high):
        return table.at[pl.ds((core * CHIPS + which_chip) * TILES + low, high - low)]

    zeros[...] = jnp.zeros_like(zeros)
    own = pltpu.make_async_copy(payload, rows_of(chip, 0, TILES), own_sem.at[0])
    own.start()
    clear = pltpu.make_async_copy(zeros, table.at[ROWS:SPAN], own_sem.at[2])
    clear.start()
    own_coef = pltpu.make_async_copy(coef, probes.at[z], own_sem.at[1])
    own_coef.start()

    def piece(f, i, j):
        _, sign, low, high = FLOWS[f]
        return rows_of(chip_at(-sign * i, -sign * j), low, high)

    def source(f, i, j):
        _, _, low, high = FLOWS[f]
        return payload.at[low:high] if i == 0 and j == 0 else piece(f, i, j)

    def push(f, i, j, along_x):
        _, sign, _, _ = FLOWS[f]
        peer = leaf_at(sign, 0) if along_x else leaf_at(0, sign)
        slot = (i + 1, j) if along_x else (i, j + 1)
        pltpu.make_async_remote_copy(
            source(f, i, j),
            piece(f, i, j),
            link_send,
            link_recv.at[f, slot[0], slot[1]],
            device_id={"leaf": peer},
            device_id_type=MESH,
        ).start()

    def share(f, i, j):
        pltpu.make_async_remote_copy(
            source(f, i, j),
            piece(f, i, j),
            chip_send,
            chip_recv,
            device_id={"leaf": twin},
            device_id_type=MESH,
        ).start()

    for t in range(NX + NY - 1):
        for i in range(NX):
            j = t - i
            if j < 0 or j >= NY:
                continue
            for f in range(4):
                x_first = FLOWS[f][0]
                if t > 0:
                    part = piece(f, i, j)
                    pltpu.make_async_copy(part, part, link_recv.at[f, i, j]).wait()
                if x_first:
                    if j == 0 and i < NX - 1:
                        push(f, i, j, True)
                    if j < NY - 1:
                        push(f, i, j, False)
                else:
                    if i == 0 and j < NY - 1:
                        push(f, i, j, False)
                    if i < NX - 1:
                        push(f, i, j, True)
                share(f, i, j)
        if t == 0:
            for s in range(1, NZ):
                pltpu.make_async_remote_copy(
                    coef,
                    probes.at[z],
                    z_send,
                    z_recv,
                    device_id={"probe": lax.rem(z + s, NZ)},
                    device_id_type=MESH,
                ).start()

    own.wait()
    own_coef.wait()
    clear.wait()
    half = table.at[0 : ROWS // 2]
    pltpu.make_async_copy(half, half, chip_recv).wait()
    pltpu.make_async_copy(half, half, chip_send).wait()
    sent = table.at[0 : (CHIPS - 1) * TILES]
    pltpu.make_async_copy(sent, sent, link_send).wait()
    others = probes.at[0 : NZ - 1]
    pltpu.make_async_copy(others, others, z_recv).wait()
    pltpu.make_async_copy(others, others, z_send).wait()


def spread(payload, coef):
    dma = pltpu.SemaphoreType.DMA
    return pl.pallas_call(
        spread_kernel,
        out_shape=(
            jax.ShapeDtypeStruct((SPAN, 16, 128), BF16),
            jax.ShapeDtypeStruct((NZ,) + coef.shape, BF16),
        ),
        in_specs=[pl.BlockSpec(memory_space=pl.ANY)] * 2,
        out_specs=[pl.BlockSpec(memory_space=TABLE_SPACE), pl.BlockSpec(memory_space=TABLE_SPACE)],
        scratch_shapes=[
            pltpu.VMEM((SPAN - ROWS, 16, 128), BF16),
            dma((4, NX, NY)),
            dma(()),
            dma(()),
            dma(()),
            dma(()),
            dma(()),
            dma((3,)),
        ],
        compiler_params=pltpu.CompilerParams(
            collective_id=0, has_side_effects=True, vmem_limit_bytes=SPREAD_LIMIT
        ),
        name="spread",
    )(payload, coef)


def take(row, index):
    return jnp.take_along_axis(jnp.broadcast_to(row, index.shape), index, axis=1)


def slot_rows(lists, slots, counts, clusters, capacity, offset, mine):
    rows = slots.shape[0]
    v = jnp.concatenate([slots, jnp.zeros((rows, 128 - PAIRS), jnp.int32)], axis=1)
    remote = jnp.maximum(v - clusters, 0)
    owner = remote // capacity
    entry = remote - owner * capacity
    found = jnp.zeros((rows, 128), jnp.int32)
    for i in range(capacity):
        found = jnp.where(entry == i, take(lists[i : i + 1], owner), found)
    is_own = v < clusters
    cluster = jnp.where(is_own, v, found)
    base = jnp.where(is_own, mine, ((owner % 2) * CHIPS + owner // 2) * TILES)
    row = base + offset + cluster // 2
    spot = lax.broadcasted_iota(jnp.int32, (rows, 128), 1)
    wide = jnp.broadcast_to(counts.astype(F32), (128, rows)).T
    live = spot.astype(F32) < wide
    row = jnp.where(live, row, ROWS)
    turn = ((cluster + spot) % 2) * 64
    return row, turn


def sweep_kernel(
    fine_slots,
    coarse_slots,
    fine_counts,
    coarse_counts,
    tiles,
    target_feats,
    probes,
    transfer,
    far,
    partial,
    stage0,
    stage1,
    staged,
    picks,
    sem,
):
    z = lax.axis_index("probe")
    leaf = lax.axis_index("leaf")
    mine = ((leaf % 2) * CHIPS + leaf // 2) * TILES

    lane = lax.broadcasted_iota(jnp.int32, (16, 128), 1)
    lists = [jnp.zeros((16, 128), F32) for _ in range(2)]
    for e in range(2 * CHIPS):
        base = ((e % 2) * CHIPS + e // 2) * TILES + HALF
        for n in range(2):
            got = pltpu.roll(tiles[base + n].astype(F32), lax.rem(e - leaf + 128, 128), 1)
            lists[n] = jnp.where(lane == e, got, lists[n])
    lists = [part.astype(jnp.int32) for part in lists]
    row, turn = slot_rows(lists[0], fine_slots[...], fine_counts[...], FINE, 16, 0, mine)
    staged[0:FINE] = row
    staged[FINE + COARSE : 2 * FINE + COARSE] = turn
    row, turn = slot_rows(
        lists[1], coarse_slots[...], coarse_counts[...], COARSE, 8, FT, mine
    )
    staged[FINE : FINE + COARSE] = row
    staged[2 * FINE + COARSE :] = turn
    move = pltpu.make_async_copy(staged, picks, sem)
    move.start()
    move.wait()

    left_half = lane < 64
    stage = (stage0, stage1)

    def gather_pair(s, p, into):
        m = 2 * p
        first = pltpu.roll(tiles[picks[s, m]], picks[FINE + COARSE + s, m], 1)
        second = pltpu.roll(tiles[picks[s, m + 1]], picks[FINE + COARSE + s, m + 1], 1)
        into[p] = jnp.where(left_half, first, second)

    def feats_of(t):
        block = target_feats[t].T
        return block[:, 0:32].astype(BF16), block[:, 32:33]

    for p in range(PAIRS // 2):
        gather_pair(FINE, p, stage0)

    def step(base, carry):
        order, packs, sides = [], [], []
        for u in range(UNROLL):
            t = base * UNROLL + u
            order += [FINE + 2 * t, 4 * t, 4 * t + 1, FINE + 2 * t + 1, 4 * t + 2, 4 * t + 3]
            packs += [feats_of(FT + t), feats_of(2 * t), feats_of(2 * t + 1)]
            n = 3 * u
            sides += [(n, 0), (n + 1, 0), (n + 1, 1), (n, 1), (n + 2, 0), (n + 2, 1)]
        order.append(FINE + 2 * jnp.minimum((base + 1) * UNROLL, CT - 1))
        totals = [None for _ in range(6 * UNROLL)]
        waiting = []

        def flush():
            for r, both, weights in waiting.pop(0):
                part = lax.dot_general(both, weights, NT, preferred_element_type=F32)
                totals[r] = part[8:16] if totals[r] is None else totals[r] + part[8:16]

        for r in range(6 * UNROLL):
            pack, half = sides[r]
            cut = slice(half * 64, half * 64 + 64)
            feats, bias = packs[pack][0][cut], packs[pack][1][cut]
            source = stage[r % 2]
            for group in range(PAIRS // (4 * BATCH)):
                batch = []
                for n in range(BATCH):
                    p = group * 2 * BATCH + n * 2
                    both = jnp.concatenate([source[p], source[p + 1]], axis=1)
                    exponent = lax.dot_general(
                        feats,
                        jnp.concatenate([both, both], axis=0),
                        (((1,), (0,)), ((), ())),
                        preferred_element_type=F32,
                    )
                    batch.append((r, both, jnp.exp2(exponent + bias).astype(BF16)))
                waiting.append(batch)
                if len(waiting) > LAG:
                    flush()
                for n in range(2 * BATCH):
                    gather_pair(order[r + 1], group * 2 * BATCH + n, stage[(r + 1) % 2])
        while waiting:
            flush()
        outs = totals
        for h in range(2 * UNROLL):
            q = base * 2 * UNROLL + h
            up, low, high = outs[3 * h : 3 * h + 3]
            cut = pl.ds(pl.multiple_of(q * 128, 128), 128)
            mats = transfer[:, cut]
            empty = jnp.zeros((8, RANK), F32)
            spread_up = jnp.concatenate(
                [
                    jnp.concatenate([up, empty], axis=1),
                    jnp.concatenate([empty, up], axis=1),
                ],
                axis=0,
            ).astype(BF16)
            down = lax.dot_general(spread_up, mats, NT, preferred_element_type=F32)
            far[:, cut] = jnp.concatenate([low + down[0:8], high + down[8:16]], axis=1)
        return carry

    lax.fori_loop(0, CT // UNROLL, step, 0)

    whole = far[...]
    first = whole.astype(BF16)
    rest = whole - first.astype(F32)
    second = rest.astype(BF16)
    third = (rest - second.astype(F32)).astype(BF16)
    coefs = probes[...].reshape(NZ * 8, FINE * RANK)
    gram = (
        lax.dot_general(coefs, first, NT, preferred_element_type=F32)
        + lax.dot_general(coefs, second, NT, preferred_element_type=F32)
        + lax.dot_general(coefs, third, NT, preferred_element_type=F32)
    )
    wide = jnp.concatenate([gram, jnp.zeros((NZ * 8, 120), F32)], axis=1)
    partial[...] = pltpu.roll(wide, z * 8, 1)


def sweep(fine_slots, coarse_slots, fine_counts, coarse_counts, table, feats, probes, transfer):
    vm = pl.BlockSpec(memory_space=pltpu.VMEM)
    return pl.pallas_call(
        sweep_kernel,
        out_shape=(
            jax.ShapeDtypeStruct((8, FINE * RANK), F32),
            jax.ShapeDtypeStruct((NZ * 8, 128), F32),
        ),
        in_specs=[vm] * 8,
        out_specs=[vm, vm],
        scratch_shapes=[
            pltpu.VMEM((PAIRS // 2, 16, 128), BF16),
            pltpu.VMEM((PAIRS // 2, 16, 128), BF16),
            pltpu.VMEM((2 * (FINE + COARSE), 128), jnp.int32),
            pltpu.SMEM((2 * (FINE + COARSE), 128), jnp.int32),
            pltpu.SemaphoreType.DMA(()),
        ],
        compiler_params=pltpu.CompilerParams(vmem_limit_bytes=SWEEP_LIMIT),
        name="sweep",
    )(fine_slots, coarse_slots, fine_counts, coarse_counts, table, feats, probes, transfer)


def reduce_kernel(gram_scale, partial, out, at_z, at_x, at_y, work, recv, send):
    leaf = lax.axis_index("leaf")
    z = lax.axis_index("probe")
    inner = lax.rem(leaf, 2 * NX)
    y = leaf // (2 * NX)

    def z_peer(s):
        return {"probe": lax.rem(z + s, NZ)}

    def x_peer(s):
        return {"leaf": y * (2 * NX) + lax.rem(inner + s, 2 * NX)}

    def y_peer(s):
        return {"leaf": lax.rem(y + s, NY) * (2 * NX) + inner}

    barrier = pltpu.get_barrier_semaphore()
    for peer in (z_peer, x_peer, y_peer):
        for s in range(1, 8):
            pl.semaphore_signal(barrier, 1, device_id=peer(s), device_id_type=MESH)
    pl.semaphore_wait(barrier, 21)

    def exchange(stage, peer, me, source, buffer):
        for s in range(1, 8):
            pltpu.make_async_remote_copy(
                source(s),
                buffer.at[me],
                send.at[stage],
                recv.at[stage],
                device_id=peer(s),
                device_id_type=MESH,
            ).start()
        buffer[me] = source(0)[...]
        got = buffer.at[0:7]
        pltpu.make_async_copy(got, got, recv.at[stage]).wait()
        total = buffer[0]
        for n in range(1, 8):
            total = total + buffer[n]
        pltpu.make_async_copy(got, got, send.at[stage]).wait()
        return total

    work[0] = exchange(0, z_peer, z, lambda s: partial.at[lax.rem(z + s, NZ)], at_z)
    work[1] = exchange(1, x_peer, inner, lambda s: work.at[0], at_x)
    out[...] = exchange(2, y_peer, y, lambda s: work.at[1], at_y) * gram_scale


def reduce_gram(partial, gram_scale):
    vm = pl.BlockSpec(memory_space=pltpu.VMEM)
    return pl.pallas_call(
        functools.partial(reduce_kernel, gram_scale),
        out_shape=jax.ShapeDtypeStruct((8, 128), F32),
        in_specs=[vm],
        out_specs=vm,
        scratch_shapes=[
            pltpu.VMEM((8, 8, 128), F32),
            pltpu.VMEM((8, 8, 128), F32),
            pltpu.VMEM((8, 8, 128), F32),
            pltpu.VMEM((2, 8, 128), F32),
            pltpu.SemaphoreType.DMA((3,)),
            pltpu.SemaphoreType.DMA((3,)),
        ],
        compiler_params=pltpu.CompilerParams(collective_id=1, has_side_effects=True),
        name="reduce_gram",
    )(partial)


def shards(
    coef_fine,
    points_fine,
    points_coarse,
    transfer,
    send_fine,
    slots_fine,
    counts_fine,
    send_coarse,
    slots_coarse,
    counts_coarse,
):
    payload, feats = prep(
        coef_fine, points_fine, points_coarse, transfer, send_fine[0].T, send_coarse[0].T
    )
    table, probes = spread(payload, coef_fine)
    far, partial = sweep(
        slots_fine,
        slots_coarse,
        counts_fine.reshape(1, FINE),
        counts_coarse.reshape(1, COARSE),
        table,
        feats,
        probes,
        transfer,
    )
    gram_scale = 1.0 / math.sqrt(2 * CHIPS * FINE * RANK)
    gram = reduce_gram(partial.reshape(NZ, 8, 128), gram_scale)
    return (far, gram[:, 0 : NZ * 8])


def solution(mesh):
    return jax.shard_map(
        shards,
        mesh=mesh,
        in_specs=(
            P("probe", "leaf"),
            P(None, "leaf"),
            P(None, "leaf"),
            P(None, "leaf"),
            P("leaf", None, None),
            P("leaf", None),
            P("leaf"),
            P("leaf", None, None),
            P("leaf", None),
            P("leaf"),
        ),
        out_specs=(P("probe", "leaf"), P("probe", None)),
        check_vma=False,
    )
```

```python
import functools
import math

import jax
import jax.numpy as jnp
from jax import lax
from jax.experimental import pallas as pl
from jax.experimental.pallas import tpu as pltpu
from jax.sharding import PartitionSpec as P

kernel_rate = 1.5
LOG2E = 1.4426950408889634
RANK = 64
NX, NY, NZ = 4, 8, 8
CHIPS = NX * NY
FINE, COARSE, PAIRS = 64, 32, 64
FT, CT = FINE // 2, COARSE // 2
HALF = FT + CT
SIZES = (CT + 2, FT)
ENDS = (2 * CHIPS * SIZES[0], 2 * CHIPS * SIZES[1])
PAD = 8
MESH = pl.DeviceIdType.MESH
F32, BF16 = jnp.float32, jnp.bfloat16
LAG = 12
LEAD = 2
EACH = 16
NT = (((1,), (1,)), ((), ()))
TABLE_SPACE = pltpu.VMEM
SPREAD_LIMIT = 20 * 1024 * 1024
SWEEP_LIMIT = 24 * 1024 * 1024


def features(points):
    high = points.astype(BF16).astype(F32)
    low = (points - high).astype(BF16).astype(F32)
    squares = points[0:1] * points[0:1] + points[1:2] * points[1:2] + points[2:3] * points[2:3]
    bias = squares * (-kernel_rate * LOG2E)
    bias_high = bias.astype(BF16).astype(F32)
    bias_low = (bias - bias_high).astype(BF16).astype(F32)
    scaled = points * (2.0 * kernel_rate * LOG2E)
    scaled_high = scaled.astype(BF16).astype(F32)
    scaled_low = (scaled - scaled_high).astype(BF16).astype(F32)
    ones = jnp.ones((2, points.shape[1]), F32)
    nothing = jnp.zeros((8, points.shape[1]), F32)
    source = jnp.concatenate([high, low, bias_high, bias_low], axis=0)
    target = jnp.concatenate(
        [
            scaled_high,
            scaled_high,
            ones,
            nothing,
            scaled_low,
            scaled_low,
            nothing[0:2],
            nothing,
            bias,
            nothing[0:7],
        ],
        axis=0,
    )
    return source, target


def prep_kernel(
    coef_in,
    fine_pts_in,
    coarse_pts_in,
    transfer_in,
    fine_list_in,
    coarse_list_in,
    fine_slots_in,
    coarse_slots_in,
    fine_counts_in,
    coarse_counts_in,
    coarse_payload,
    fine_payload,
    target_out,
    codes,
    coef,
    transfer,
    fine_pts,
    coarse_pts,
    fine_list,
    coarse_list,
    fine_slots,
    coarse_slots,
    fine_counts,
    coarse_counts,
    sems,
):
    moves = [
        (fine_pts_in, fine_pts),
        (coef_in, coef),
        (transfer_in, transfer),
        (coarse_pts_in, coarse_pts),
        (fine_list_in, fine_list),
        (coarse_list_in, coarse_list),
        (fine_slots_in, fine_slots),
        (coarse_slots_in, coarse_slots),
        (fine_counts_in, fine_counts),
        (coarse_counts_in, coarse_counts),
    ]
    copies = [pltpu.make_async_copy(a, b, sems.at[n]) for n, (a, b) in enumerate(moves)]
    for copy in copies:
        copy.start()
    copies[0].wait()
    copies[1].wait()
    source, target = features(fine_pts[...])
    for t in range(FT):
        cut = slice(t * 128, t * 128 + 128)
        rows = jnp.concatenate([source[:, cut], coef[:, cut].astype(F32)], axis=0)
        fine_payload[t] = rows.astype(BF16)
        target_out[t] = target[:, cut]
    for copy in copies[2:]:
        copy.wait()
    source, target = features(coarse_pts[...])
    for t in range(CT):
        halves = []
        for q in (2 * t, 2 * t + 1):
            mats = transfer[:, q * 128 : q * 128 + 128]
            left = jnp.dot(
                coef[:, q * 128 : q * 128 + 64], mats, preferred_element_type=F32
            )
            right = jnp.dot(
                coef[:, q * 128 + 64 : q * 128 + 128], mats, preferred_element_type=F32
            )
            halves.append(left[:, 0:64] + right[:, 64:128])
        cut = slice(t * 128, t * 128 + 128)
        rows = jnp.concatenate([source[:, cut], jnp.concatenate(halves, axis=1)], axis=0)
        coarse_payload[t] = rows.astype(BF16)
        target_out[FT + t] = target[:, cut]
    entries = [fine_list[...].astype(F32), coarse_list[...].astype(F32), jnp.zeros((8, 64), F32)]
    for n in range(2):
        part = entries[0] if n == 0 else jnp.concatenate(entries[1:], axis=0)
        coarse_payload[CT + n] = jnp.concatenate([part, jnp.zeros((16, 64), F32)], axis=1).astype(BF16)
    for slots, counts, at in ((fine_slots, fine_counts, 0), (coarse_slots, coarse_counts, FINE)):
        rows = slots.shape[0]
        wide = jnp.broadcast_to(counts[...].astype(F32), (128, rows)).T
        spot = lax.broadcasted_iota(jnp.int32, (rows, 128), 1)
        code = jnp.concatenate([slots[...], jnp.zeros((rows, 128 - PAIRS), jnp.int32)], axis=1)
        codes[at : at + rows] = jnp.where(spot.astype(F32) < wide, code, -1)


def prep(*arrays):
    vm = pl.BlockSpec(memory_space=pltpu.VMEM)
    kept = (0, 3)
    return pl.pallas_call(
        prep_kernel,
        out_shape=(
            jax.ShapeDtypeStruct((SIZES[0], 16, 128), BF16),
            jax.ShapeDtypeStruct((SIZES[1], 16, 128), BF16),
            jax.ShapeDtypeStruct((HALF, 40, 128), F32),
            jax.ShapeDtypeStruct((FINE + COARSE, 128), jnp.int32),
        )
        + tuple(jax.ShapeDtypeStruct(arrays[n].shape, arrays[n].dtype) for n in kept),
        in_specs=[pl.BlockSpec(memory_space=pltpu.HBM)] * len(arrays),
        out_specs=[vm] * 6,
        scratch_shapes=[
            pltpu.VMEM(array.shape, array.dtype)
            for n, array in enumerate(arrays)
            if n not in kept
        ]
        + [pltpu.SemaphoreType.DMA((len(arrays),))],
        compiler_params=pltpu.CompilerParams(vmem_limit_bytes=8 * 1024 * 1024),
        name="prep",
    )(*arrays)


def take(row, index):
    return jnp.take_along_axis(jnp.broadcast_to(row, index.shape), index, axis=1)


def slot_rows(lists, code, clusters, capacity, level, owner_slot):
    live = code >= 0
    v = jnp.maximum(code, 0)
    remote = jnp.maximum(v - clusters, 0)
    owner = remote // capacity
    entry = remote - owner * capacity
    found = jnp.zeros(code.shape, jnp.int32)
    for i in range(capacity):
        found = jnp.where(entry == i, take(lists[i : i + 1], owner), found)
    is_own = v < clusters
    cluster = jnp.where(is_own, v, found)
    base = jnp.where(is_own, owner_slot, (owner % 2) * CHIPS + owner // 2) * SIZES[level]
    row = jnp.where(live, base + cluster // 2, ENDS[level])
    spot = lax.broadcasted_iota(jnp.int32, code.shape, 1)
    turn = ((cluster + spot) % 2) * 64
    return row, turn


def list_part(tiles, n, leaf):
    lane = lax.broadcasted_iota(jnp.int32, (16, 128), 1)
    part = jnp.zeros((16, 128), F32)
    for e in range(2 * CHIPS):
        base = ((e % 2) * CHIPS + e // 2) * SIZES[0] + CT
        got = pltpu.roll(tiles[base + n].astype(F32), lax.rem(e - leaf + 128, 128), 1)
        part = jnp.where(lane == e, got, part)
    return part.astype(jnp.int32)


def gather_pair(tiles, picks, count, s, p, into):
    m = 2 * p
    lane = lax.broadcasted_iota(jnp.int32, (16, 128), 1)
    first = pltpu.roll(tiles[picks[s, m]], picks[count + s, m], 1)
    second = pltpu.roll(tiles[picks[s, m + 1]], picks[count + s, m + 1], 1)
    into[p] = jnp.where(lane < 64, first, second)


def gather_all(tiles, picks, count, s, into):
    for p in range(PAIRS // 2):
        gather_pair(tiles, picks, count, s, p, into)


def feats_of(target_feats, t):
    block = target_feats[t].T
    feats, bias = block[:, 0:32].astype(BF16), block[:, 32:33]
    return [(feats[cut], bias[cut]) for cut in (slice(0, 64), slice(64, 128))]


def run_targets(tiles, picks, count, order, targets, stage):
    totals = [None for _ in targets]
    waiting = []

    def flush():
        r, both, weights = waiting.pop(0)
        part = lax.dot_general(both, weights, NT, preferred_element_type=F32)
        totals[r] = part[8:16] if totals[r] is None else totals[r] + part[8:16]

    for r, (feats, bias) in enumerate(targets):
        source = stage[r % 2]
        for group in range(PAIRS // 4):
            p = group * 2
            both = jnp.concatenate([source[p], source[p + 1]], axis=1)
            exponent = lax.dot_general(
                feats,
                jnp.concatenate([both, both], axis=0),
                (((1,), (0,)), ((), ())),
                preferred_element_type=F32,
            )
            waiting.append((r, both, jnp.exp2(exponent + bias).astype(BF16)))
            if len(waiting) > LAG:
                flush()
            for n in range(2):
                gather_pair(tiles, picks, count, order[r + 1], p + n, stage[(r + 1) % 2])
    while waiting:
        flush()
    return totals


FLOWS = (
    (True, 1, 0, 4),
    (True, -1, 4, 8),
    (False, 1, 8, 13),
    (False, -1, 13, 18),
    (True, 1, 0, 7),
    (True, -1, 7, 13),
    (False, 1, 13, 23),
    (False, -1, 23, 32),
)


def spread_kernel(
    coarse_payload,
    fine_payload,
    coef,
    target_feats,
    codes,
    fine_table,
    probes,
    staged,
    coarse_out,
    coarse_table,
    coarse_staged,
    zeros,
    stage0,
    stage1,
    picks,
    link_recv,
    link_send,
    chip_recv,
    chip_send,
    z_recv,
    z_send,
    own_sem,
):
    leaf = lax.axis_index("leaf")
    z = lax.axis_index("probe")
    core = lax.rem(leaf, 2)
    chip = leaf // 2
    x = lax.rem(chip, NX)
    y = chip // NX

    def chip_at(xs, ys):
        return lax.rem(y + ys + NY, NY) * NX + lax.rem(x + xs + NX, NX)

    def leaf_at(xs, ys):
        return chip_at(xs, ys) * 2 + core

    twin = chip * 2 + (1 - core)
    barrier = pltpu.get_barrier_semaphore()
    peers = [leaf_at(1, 0), leaf_at(-1, 0), leaf_at(0, 1), leaf_at(0, -1), twin]
    for peer in peers:
        pl.semaphore_signal(barrier, 1, device_id={"leaf": peer}, device_id_type=MESH)
    for s in range(1, NZ):
        pl.semaphore_signal(
            barrier, 1, device_id={"probe": lax.rem(z + s, NZ)}, device_id_type=MESH
        )
    pl.semaphore_wait(barrier, len(peers) + NZ - 1)

    payloads, tables = (coarse_payload, fine_payload), (coarse_table, fine_table)

    def rows_of(level, which_chip, low, high):
        first = (core * CHIPS + which_chip) * SIZES[level] + low
        return tables[level].at[pl.ds(first, high - low)]

    zeros[...] = jnp.zeros_like(zeros)
    local = []
    for level in range(2):
        end = ENDS[level]
        local.append((payloads[level], rows_of(level, chip, 0, SIZES[level])))
        local.append((zeros, tables[level].at[end : end + PAD]))
    local = [pltpu.make_async_copy(a, b, own_sem.at[n]) for n, (a, b) in enumerate(local)]
    for copy in local:
        copy.start()
    own_coef = pltpu.make_async_copy(coef, probes.at[z], own_sem.at[4])
    own_coef.start()

    def share_bytes(sem, which_core, level):
        count = CHIPS * SIZES[level]
        block = tables[level].at[pl.ds(which_core * count, count)]
        pltpu.make_async_copy(block, block, sem).wait()

    def piece(f, i, j):
        _, sign, low, high = FLOWS[f]
        return rows_of(f // 4, chip_at(-sign * i, -sign * j), low, high)

    def source(f, i, j):
        _, _, low, high = FLOWS[f]
        own_piece = isinstance(j, int) and i == 0 and j == 0
        return payloads[f // 4].at[low:high] if own_piece else piece(f, i, j)

    def push(f, i, j, along_x):
        _, sign, _, _ = FLOWS[f]
        peer = leaf_at(sign, 0) if along_x else leaf_at(0, sign)
        slot = (i + 1, j) if along_x else (i, j + 1)
        pltpu.make_async_remote_copy(
            source(f, i, j),
            piece(f, i, j),
            link_send.at[f // 4],
            link_recv.at[f, slot[0], slot[1]],
            device_id={"leaf": peer},
            device_id_type=MESH,
        ).start()

    def share(f, i, j):
        pltpu.make_async_remote_copy(
            source(f, i, j),
            piece(f, i, j),
            chip_send.at[f // 4],
            chip_recv.at[f // 4],
            device_id={"leaf": twin},
            device_id_type=MESH,
        ).start()

    def visit(f, i, j, arrived):
        if arrived:
            part = piece(f, i, j)
            pltpu.make_async_copy(part, part, link_recv.at[f, i, j]).wait()
        more_y = NY - 1 > j
        if FLOWS[f][0]:
            if i < NX - 1:
                pl.when(j == 0)(lambda: push(f, i, j, True))
            pl.when(more_y)(lambda: push(f, i, j, False))
        else:
            if i == 0:
                pl.when(more_y)(lambda: push(f, i, j, False))
            if i < NX - 1:
                push(f, i, j, True)
        share(f, i, j)

    def wave(flows, t):
        for i in range(NX):
            j = t - i
            if isinstance(t, int):
                if 0 <= j < NY:
                    for f in flows:
                        visit(f, i, j, t > 0)
            else:

                @pl.when(jnp.logical_and(j >= 0, j < NY))
                def _():
                    for f in flows:
                        visit(f, i, j, True)

    early, late = range(4), range(4, 8)
    wave(early, 0)
    wave(late, 0)
    for s in range(1, NZ):
        pltpu.make_async_remote_copy(
            coef,
            probes.at[z],
            z_send,
            z_recv,
            device_id={"probe": lax.rem(z + s, NZ)},
            device_id_type=MESH,
        ).start()
    for t in range(1, NX + NY - 1):
        wave(early, t)
        if t >= NX + NY - 1 - LEAD:
            wave(late, t - (NX + NY - 2 - LEAD))
    for copy in local:
        copy.wait()
    share_bytes(chip_recv.at[0], 1 - core, 0)

    owner_slot = core * CHIPS + chip
    lists = [list_part(coarse_table, n, leaf) for n in range(2)]
    row, turn = slot_rows(lists[1], codes[FINE:], COARSE, 8, 0, owner_slot)
    coarse_staged[0:COARSE] = row
    coarse_staged[COARSE:] = turn
    move = pltpu.make_async_copy(coarse_staged, picks, own_sem.at[5])
    move.start()
    row, turn = slot_rows(lists[0], codes[0:FINE], FINE, 16, 1, owner_slot)
    staged[0:FINE] = row
    staged[FINE:] = turn
    move.wait()
    stage = (stage0, stage1)
    gather_all(coarse_table, picks, COARSE, 0, stage0)
    steps = NX + NY - 2 - LEAD
    each = COARSE // steps

    def body(n, carry):
        wave(late, n + LEAD + 1)
        order = [n * each + u for u in range(each)]
        order.append(jnp.minimum((n + 1) * each, COARSE - 1))
        targets = []
        for u in range(each // 2):
            targets += feats_of(target_feats, FT + n * (each // 2) + u)
        outs = run_targets(coarse_table, picks, COARSE, order, targets, stage)
        for u in range(each):
            coarse_out[n * each + u] = jnp.concatenate(
                [outs[u], jnp.zeros((8, RANK), F32)], axis=1
            )
        return carry

    lax.fori_loop(0, steps, body, 0)

    own_coef.wait()
    share_bytes(chip_recv.at[1], 1 - core, 1)
    for level in range(2):
        share_bytes(chip_send.at[level], core, level)
        sent = tables[level].at[0 : (CHIPS - 1) * SIZES[level]]
        pltpu.make_async_copy(sent, sent, link_send.at[level]).wait()
    others = probes.at[0 : NZ - 1]
    pltpu.make_async_copy(others, others, z_recv).wait()
    pltpu.make_async_copy(others, others, z_send).wait()


def spread(coarse_payload, fine_payload, coef, feats, codes):
    dma = pltpu.SemaphoreType.DMA
    vm = pl.BlockSpec(memory_space=pltpu.VMEM)
    return pl.pallas_call(
        spread_kernel,
        out_shape=(
            jax.ShapeDtypeStruct((ENDS[1] + PAD, 16, 128), BF16),
            jax.ShapeDtypeStruct((NZ,) + coef.shape, BF16),
            jax.ShapeDtypeStruct((2 * FINE, 128), jnp.int32),
            jax.ShapeDtypeStruct((COARSE, 8, 128), F32),
        ),
        in_specs=[vm] * 5,
        out_specs=[vm] * 4,
        scratch_shapes=[
            pltpu.VMEM((ENDS[0] + PAD, 16, 128), BF16),
            pltpu.VMEM((2 * COARSE, 128), jnp.int32),
            pltpu.VMEM((PAD, 16, 128), BF16),
            pltpu.VMEM((PAIRS // 2, 16, 128), BF16),
            pltpu.VMEM((PAIRS // 2, 16, 128), BF16),
            pltpu.SMEM((2 * COARSE, 128), jnp.int32),
            dma((8, NX, NY)),
            dma((2,)),
            dma((2,)),
            dma((2,)),
            dma(()),
            dma(()),
            dma((6,)),
        ],
        compiler_params=pltpu.CompilerParams(
            collective_id=0, has_side_effects=True, vmem_limit_bytes=SPREAD_LIMIT
        ),
        name="spread",
    )(coarse_payload, fine_payload, coef, feats, codes)


def sweep_kernel(
    staged, tiles, target_feats, probes, transfer, coarse, far, partial, stage0, stage1, picks, sem
):
    z = lax.axis_index("probe")
    move = pltpu.make_async_copy(staged, picks, sem)
    move.start()
    move.wait()
    stage = (stage0, stage1)
    gather_all(tiles, picks, FINE, 0, stage0)

    def step(n, carry):
        order = [n * EACH + u for u in range(EACH)]
        order.append(jnp.minimum((n + 1) * EACH, FINE - 1))
        targets = []
        for u in range(EACH // 2):
            targets += feats_of(target_feats, n * (EACH // 2) + u)
        outs = run_targets(tiles, picks, FINE, order, targets, stage)
        for u in range(EACH // 2):
            q = n * (EACH // 2) + u
            cut = pl.ds(pl.multiple_of(q * 128, 128), 128)
            mats = transfer[:, cut]
            up = coarse[q]
            spread_up = jnp.concatenate([up, pltpu.roll(up, RANK, 1)], axis=0).astype(BF16)
            down = lax.dot_general(spread_up, mats, NT, preferred_element_type=F32)
            low, high = outs[2 * u : 2 * u + 2]
            far[:, cut] = jnp.concatenate([low + down[0:8], high + down[8:16]], axis=1)
        return carry

    lax.fori_loop(0, FINE // EACH, step, 0)

    whole = far[...]
    first = whole.astype(BF16)
    rest = whole - first.astype(F32)
    second = rest.astype(BF16)
    third = (rest - second.astype(F32)).astype(BF16)
    coefs = probes[...].reshape(NZ * 8, FINE * RANK)
    gram = (
        lax.dot_general(coefs, first, NT, preferred_element_type=F32)
        + lax.dot_general(coefs, second, NT, preferred_element_type=F32)
        + lax.dot_general(coefs, third, NT, preferred_element_type=F32)
    )
    wide = jnp.concatenate([gram, jnp.zeros((NZ * 8, 120), F32)], axis=1)
    partial[...] = pltpu.roll(wide, z * 8, 1)


def sweep(staged, table, feats, probes, transfer, coarse):
    vm = pl.BlockSpec(memory_space=pltpu.VMEM)
    return pl.pallas_call(
        sweep_kernel,
        out_shape=(
            jax.ShapeDtypeStruct((8, FINE * RANK), F32),
            jax.ShapeDtypeStruct((NZ * 8, 128), F32),
        ),
        in_specs=[vm] * 6,
        out_specs=[vm, vm],
        scratch_shapes=[
            pltpu.VMEM((PAIRS // 2, 16, 128), BF16),
            pltpu.VMEM((PAIRS // 2, 16, 128), BF16),
            pltpu.SMEM((2 * FINE, 128), jnp.int32),
            pltpu.SemaphoreType.DMA(()),
        ],
        compiler_params=pltpu.CompilerParams(vmem_limit_bytes=SWEEP_LIMIT),
        name="sweep",
    )(staged, table, feats, probes, transfer, coarse)


def reduce_kernel(gram_scale, partial, out, at_z, at_x, at_y, work, recv, send):
    leaf = lax.axis_index("leaf")
    z = lax.axis_index("probe")
    inner = lax.rem(leaf, 2 * NX)
    y = leaf // (2 * NX)

    def z_peer(s):
        return {"probe": lax.rem(z + s, NZ)}

    def x_peer(s):
        return {"leaf": y * (2 * NX) + lax.rem(inner + s, 2 * NX)}

    def y_peer(s):
        return {"leaf": lax.rem(y + s, NY) * (2 * NX) + inner}

    barrier = pltpu.get_barrier_semaphore()
    for peer in (z_peer, x_peer, y_peer):
        for s in range(1, 8):
            pl.semaphore_signal(barrier, 1, device_id=peer(s), device_id_type=MESH)
    pl.semaphore_wait(barrier, 21)

    def exchange(stage, peer, me, source, buffer):
        for s in range(1, 8):
            pltpu.make_async_remote_copy(
                source(s),
                buffer.at[me],
                send.at[stage],
                recv.at[stage],
                device_id=peer(s),
                device_id_type=MESH,
            ).start()
        buffer[me] = source(0)[...]
        got = buffer.at[0:7]
        pltpu.make_async_copy(got, got, recv.at[stage]).wait()
        total = buffer[0]
        for n in range(1, 8):
            total = total + buffer[n]
        pltpu.make_async_copy(got, got, send.at[stage]).wait()
        return total

    work[0] = exchange(0, z_peer, z, lambda s: partial.at[lax.rem(z + s, NZ)], at_z)
    work[1] = exchange(1, x_peer, inner, lambda s: work.at[0], at_x)
    out[...] = exchange(2, y_peer, y, lambda s: work.at[1], at_y) * gram_scale


def reduce_gram(partial, gram_scale):
    vm = pl.BlockSpec(memory_space=pltpu.VMEM)
    return pl.pallas_call(
        functools.partial(reduce_kernel, gram_scale),
        out_shape=jax.ShapeDtypeStruct((8, 128), F32),
        in_specs=[vm],
        out_specs=vm,
        scratch_shapes=[
            pltpu.VMEM((8, 8, 128), F32),
            pltpu.VMEM((8, 8, 128), F32),
            pltpu.VMEM((8, 8, 128), F32),
            pltpu.VMEM((2, 8, 128), F32),
            pltpu.SemaphoreType.DMA((3,)),
            pltpu.SemaphoreType.DMA((3,)),
        ],
        compiler_params=pltpu.CompilerParams(
            collective_id=1, has_side_effects=True, vmem_limit_bytes=1024 * 1024
        ),
        name="reduce_gram",
    )(partial)


def shards(
    coef_fine,
    points_fine,
    points_coarse,
    transfer,
    send_fine,
    slots_fine,
    counts_fine,
    send_coarse,
    slots_coarse,
    counts_coarse,
):
    arrays = (
        coef_fine,
        points_fine,
        points_coarse,
        transfer,
        send_fine[0].T,
        send_coarse[0].T,
        slots_fine,
        slots_coarse,
        counts_fine.reshape(1, FINE),
        counts_coarse.reshape(1, COARSE),
    )
    coarse_payload, fine_payload, feats, codes, coef, mats = prep(
        *[pltpu.with_memory_space_constraint(array, pltpu.HBM) for array in arrays]
    )
    table, probes, staged, coarse = spread(coarse_payload, fine_payload, coef, feats, codes)
    far, partial = sweep(staged, table, feats, probes, mats, coarse)
    gram_scale = 1.0 / math.sqrt(2 * CHIPS * FINE * RANK)
    gram = reduce_gram(partial.reshape(NZ, 8, 128), gram_scale)
    return (far, gram[:, 0 : NZ * 8])


def solution(mesh):
    return jax.shard_map(
        shards,
        mesh=mesh,
        in_specs=(
            P("probe", "leaf"),
            P(None, "leaf"),
            P(None, "leaf"),
            P(None, "leaf"),
            P("leaf", None, None),
            P("leaf", None),
            P("leaf"),
            P("leaf", None, None),
            P("leaf", None),
            P("leaf"),
        ),
        out_specs=(P("probe", "leaf"), P("probe", None)),
        check_vma=False,
    )
```

```python
import functools
import math

import jax
import jax.numpy as jnp
from jax import lax
from jax.experimental import pallas as pl
from jax.experimental.pallas import tpu as pltpu
from jax.sharding import PartitionSpec as P

kernel_rate = 1.5
LOG2E = 1.4426950408889634
RANK = 64
NX, NY, NZ = 4, 8, 8
CHIPS = NX * NY
FINE, COARSE, PAIRS = 64, 32, 64
FT, CT = FINE // 2, COARSE // 2
HALF = FT + CT
SIZES = (CT + 2, FT)
ENDS = (2 * CHIPS * SIZES[0], 2 * CHIPS * SIZES[1])
PAD = 8
MESH = pl.DeviceIdType.MESH
F32, BF16 = jnp.float32, jnp.bfloat16
LAG = 12
EACH = 16
X_TREE = {1: 0, 2: 1, -1: 0}
Y_TREE = {1: 0, 2: 1, 3: 2, 4: 3, -1: 0, -2: -1, -3: -2}
COARSE_WAVE, FINE_WAVE, COMPUTE = 0, 1, 2
SCHEDULE = (
    (COARSE_WAVE, 0),
    (FINE_WAVE, 0),
    (COARSE_WAVE, 1),
    (COARSE_WAVE, 2),
    (FINE_WAVE, 1),
    (COARSE_WAVE, 3),
    (COARSE_WAVE, 4),
    (FINE_WAVE, 2),
    (COARSE_WAVE, 5),
    (COARSE_WAVE, 6),
    (FINE_WAVE, 3),
    (COMPUTE, 3),
    (FINE_WAVE, 4),
    (COMPUTE, 3),
    (FINE_WAVE, 5),
    (COMPUTE, 2),
    (FINE_WAVE, 6),
)
CHUNK = 4
NT = (((1,), (1,)), ((), ()))
TABLE_SPACE = pltpu.VMEM
SPREAD_LIMIT = 20 * 1024 * 1024
SWEEP_LIMIT = 24 * 1024 * 1024


def features(points):
    high = points.astype(BF16).astype(F32)
    low = (points - high).astype(BF16).astype(F32)
    squares = points[0:1] * points[0:1] + points[1:2] * points[1:2] + points[2:3] * points[2:3]
    bias = squares * (-kernel_rate * LOG2E)
    bias_high = bias.astype(BF16).astype(F32)
    bias_low = (bias - bias_high).astype(BF16).astype(F32)
    scaled = points * (2.0 * kernel_rate * LOG2E)
    scaled_high = scaled.astype(BF16).astype(F32)
    scaled_low = (scaled - scaled_high).astype(BF16).astype(F32)
    ones = jnp.ones((2, points.shape[1]), F32)
    nothing = jnp.zeros((8, points.shape[1]), F32)
    source = jnp.concatenate([high, low, bias_high, bias_low], axis=0)
    target = jnp.concatenate(
        [
            scaled_high,
            scaled_high,
            ones,
            nothing,
            scaled_low,
            scaled_low,
            nothing[0:2],
            nothing,
            bias,
            nothing[0:7],
        ],
        axis=0,
    )
    return source, target


def prep_kernel(
    coef_in,
    fine_pts_in,
    coarse_pts_in,
    transfer_in,
    fine_list_in,
    coarse_list_in,
    fine_slots_in,
    coarse_slots_in,
    fine_counts_in,
    coarse_counts_in,
    coarse_payload,
    fine_payload,
    target_out,
    codes,
    coef,
    transfer,
    fine_pts,
    coarse_pts,
    fine_list,
    coarse_list,
    fine_slots,
    coarse_slots,
    fine_counts,
    coarse_counts,
    sems,
):
    moves = [
        (fine_pts_in, fine_pts),
        (coef_in, coef),
        (transfer_in, transfer),
        (coarse_pts_in, coarse_pts),
        (fine_list_in, fine_list),
        (coarse_list_in, coarse_list),
        (fine_slots_in, fine_slots),
        (coarse_slots_in, coarse_slots),
        (fine_counts_in, fine_counts),
        (coarse_counts_in, coarse_counts),
    ]
    copies = [pltpu.make_async_copy(a, b, sems.at[n]) for n, (a, b) in enumerate(moves)]
    for copy in copies:
        copy.start()
    copies[0].wait()
    copies[1].wait()
    source, target = features(fine_pts[...])
    for t in range(FT):
        cut = slice(t * 128, t * 128 + 128)
        rows = jnp.concatenate([source[:, cut], coef[:, cut].astype(F32)], axis=0)
        fine_payload[t] = rows.astype(BF16)
        target_out[t] = target[:, cut]
    for copy in copies[2:]:
        copy.wait()
    source, target = features(coarse_pts[...])
    for t in range(CT):
        halves = []
        for q in (2 * t, 2 * t + 1):
            mats = transfer[:, q * 128 : q * 128 + 128]
            left = jnp.dot(
                coef[:, q * 128 : q * 128 + 64], mats, preferred_element_type=F32
            )
            right = jnp.dot(
                coef[:, q * 128 + 64 : q * 128 + 128], mats, preferred_element_type=F32
            )
            halves.append(left[:, 0:64] + right[:, 64:128])
        cut = slice(t * 128, t * 128 + 128)
        rows = jnp.concatenate([source[:, cut], jnp.concatenate(halves, axis=1)], axis=0)
        coarse_payload[t] = rows.astype(BF16)
        target_out[FT + t] = target[:, cut]
    entries = [fine_list[...].astype(F32), coarse_list[...].astype(F32), jnp.zeros((8, 64), F32)]
    for n in range(2):
        part = entries[0] if n == 0 else jnp.concatenate(entries[1:], axis=0)
        coarse_payload[CT + n] = jnp.concatenate([part, jnp.zeros((16, 64), F32)], axis=1).astype(BF16)
    for slots, counts, at in ((fine_slots, fine_counts, 0), (coarse_slots, coarse_counts, FINE)):
        rows = slots.shape[0]
        wide = jnp.broadcast_to(counts[...].astype(F32), (128, rows)).T
        spot = lax.broadcasted_iota(jnp.int32, (rows, 128), 1)
        code = jnp.concatenate([slots[...], jnp.zeros((rows, 128 - PAIRS), jnp.int32)], axis=1)
        codes[at : at + rows] = jnp.where(spot.astype(F32) < wide, code, -1)


def prep(*arrays):
    vm = pl.BlockSpec(memory_space=pltpu.VMEM)
    kept = (0, 3)
    return pl.pallas_call(
        prep_kernel,
        out_shape=(
            jax.ShapeDtypeStruct((SIZES[0], 16, 128), BF16),
            jax.ShapeDtypeStruct((SIZES[1], 16, 128), BF16),
            jax.ShapeDtypeStruct((HALF, 40, 128), F32),
            jax.ShapeDtypeStruct((FINE + COARSE, 128), jnp.int32),
        )
        + tuple(jax.ShapeDtypeStruct(arrays[n].shape, arrays[n].dtype) for n in kept),
        in_specs=[pl.BlockSpec(memory_space=pltpu.HBM)] * len(arrays),
        out_specs=[vm] * 6,
        scratch_shapes=[
            pltpu.VMEM(array.shape, array.dtype)
            for n, array in enumerate(arrays)
            if n not in kept
        ]
        + [pltpu.SemaphoreType.DMA((len(arrays),))],
        compiler_params=pltpu.CompilerParams(vmem_limit_bytes=8 * 1024 * 1024),
        name="prep",
    )(*arrays)


def take(row, index):
    return jnp.take_along_axis(jnp.broadcast_to(row, index.shape), index, axis=1)


def slot_rows(lists, code, clusters, capacity, level, owner_slot):
    live = code >= 0
    v = jnp.maximum(code, 0)
    remote = jnp.maximum(v - clusters, 0)
    owner = remote // capacity
    entry = remote - owner * capacity
    found = jnp.zeros(code.shape, jnp.int32)
    for i in range(capacity):
        found = jnp.where(entry == i, take(lists[i : i + 1], owner), found)
    is_own = v < clusters
    cluster = jnp.where(is_own, v, found)
    base = jnp.where(is_own, owner_slot, (owner % 2) * CHIPS + owner // 2) * SIZES[level]
    row = jnp.where(live, base + cluster // 2, ENDS[level])
    spot = lax.broadcasted_iota(jnp.int32, code.shape, 1)
    turn = ((cluster + spot) % 2) * 64
    return row, turn


def list_part(tiles, n, leaf):
    lane = lax.broadcasted_iota(jnp.int32, (16, 128), 1)
    part = jnp.zeros((16, 128), F32)
    for e in range(2 * CHIPS):
        base = ((e % 2) * CHIPS + e // 2) * SIZES[0] + CT
        got = pltpu.roll(tiles[base + n].astype(F32), lax.rem(e - leaf + 128, 128), 1)
        part = jnp.where(lane == e, got, part)
    return part.astype(jnp.int32)


def gather_pair(tiles, picks, count, s, p, into):
    m = 2 * p
    lane = lax.broadcasted_iota(jnp.int32, (16, 128), 1)
    first = pltpu.roll(tiles[picks[s, m]], picks[count + s, m], 1)
    second = pltpu.roll(tiles[picks[s, m + 1]], picks[count + s, m + 1], 1)
    into[p] = jnp.where(lane < 64, first, second)


def gather_all(tiles, picks, count, s, into):
    for p in range(PAIRS // 2):
        gather_pair(tiles, picks, count, s, p, into)


def feats_of(target_feats, t):
    block = target_feats[t].T
    feats, bias = block[:, 0:32].astype(BF16), block[:, 32:33]
    return [(feats[cut], bias[cut]) for cut in (slice(0, 64), slice(64, 128))]


def run_targets(tiles, picks, count, order, targets, stage):
    totals = [None for _ in targets]
    waiting = []

    def flush():
        r, both, weights = waiting.pop(0)
        part = lax.dot_general(both, weights, NT, preferred_element_type=F32)
        totals[r] = part[8:16] if totals[r] is None else totals[r] + part[8:16]

    for r, (feats, bias) in enumerate(targets):
        source = stage[r % 2]
        for group in range(PAIRS // 4):
            p = group * 2
            both = jnp.concatenate([source[p], source[p + 1]], axis=1)
            exponent = lax.dot_general(
                feats,
                jnp.concatenate([both, both], axis=0),
                (((1,), (0,)), ((), ())),
                preferred_element_type=F32,
            )
            waiting.append((r, both, jnp.exp2(exponent + bias).astype(BF16)))
            if len(waiting) > LAG:
                flush()
            for n in range(2):
                gather_pair(tiles, picks, count, order[r + 1], p + n, stage[(r + 1) % 2])
    while waiting:
        flush()
    return totals


FLOWS = (
    (True, 1, 0, 4),
    (True, -1, 4, 8),
    (False, 1, 8, 13),
    (False, -1, 13, 18),
    (True, 1, 0, 7),
    (True, -1, 7, 13),
    (False, 1, 13, 23),
    (False, -1, 23, 32),
)


def children(tree, offset):
    return [child - offset for child, parent in tree.items() if parent == offset]


def spread_kernel(
    coarse_payload,
    fine_payload,
    coef,
    target_feats,
    codes,
    fine_table,
    probes,
    staged,
    coarse_out,
    coarse_table,
    coarse_staged,
    zeros,
    stage0,
    stage1,
    picks,
    link_recv,
    link_send,
    chip_recv,
    chip_send,
    z_recv,
    z_send,
    own_sem,
):
    leaf = lax.axis_index("leaf")
    z = lax.axis_index("probe")
    core = lax.rem(leaf, 2)
    chip = leaf // 2
    x = lax.rem(chip, NX)
    y = chip // NX

    def chip_at(xs, ys):
        return lax.rem(y + ys + NY, NY) * NX + lax.rem(x + xs + NX, NX)

    def leaf_at(xs, ys):
        return chip_at(xs, ys) * 2 + core

    twin = chip * 2 + (1 - core)
    barrier = pltpu.get_barrier_semaphore()
    peers = [leaf_at(1, 0), leaf_at(-1, 0), leaf_at(0, 1), leaf_at(0, -1), twin]
    for peer in peers:
        pl.semaphore_signal(barrier, 1, device_id={"leaf": peer}, device_id_type=MESH)
    for s in range(1, NZ):
        pl.semaphore_signal(
            barrier, 1, device_id={"probe": lax.rem(z + s, NZ)}, device_id_type=MESH
        )
    pl.semaphore_wait(barrier, len(peers) + NZ - 1)

    payloads, tables = (coarse_payload, fine_payload), (coarse_table, fine_table)

    def rows_of(level, which_chip, low, high):
        first = (core * CHIPS + which_chip) * SIZES[level] + low
        return tables[level].at[pl.ds(first, high - low)]

    zeros[...] = jnp.zeros_like(zeros)
    local = []
    for level in range(2):
        end = ENDS[level]
        local.append((payloads[level], rows_of(level, chip, 0, SIZES[level])))
        local.append((zeros, tables[level].at[end : end + PAD]))
    local = [pltpu.make_async_copy(a, b, own_sem.at[n]) for n, (a, b) in enumerate(local)]
    for copy in local:
        copy.start()
    own_coef = pltpu.make_async_copy(coef, probes.at[z], own_sem.at[4])
    own_coef.start()

    def share_bytes(sem, which_core, level):
        count = CHIPS * SIZES[level]
        block = tables[level].at[pl.ds(which_core * count, count)]
        pltpu.make_async_copy(block, block, sem).wait()

    def piece(f, i, j):
        _, sign, low, high = FLOWS[f]
        return rows_of(f // 4, chip_at(-sign * i, -sign * j), low, high)

    def source(f, i, j):
        _, _, low, high = FLOWS[f]
        return payloads[f // 4].at[low:high] if i == 0 and j == 0 else piece(f, i, j)

    def push(f, i, j, along_x, hop):
        step = FLOWS[f][1] * hop
        peer = leaf_at(step, 0) if along_x else leaf_at(0, step)
        slot = (i + hop, j) if along_x else (i, j + hop)
        pltpu.make_async_remote_copy(
            source(f, i, j),
            piece(f, i, j),
            link_send.at[f // 4],
            link_recv.at[f, slot[0] + 1, slot[1] + 3],
            device_id={"leaf": peer},
            device_id_type=MESH,
        ).start()

    def share(f, i, j):
        pltpu.make_async_remote_copy(
            source(f, i, j),
            piece(f, i, j),
            chip_send.at[f // 4],
            chip_recv.at[f // 4],
            device_id={"leaf": twin},
            device_id_type=MESH,
        ).start()

    def visit(f, i, j):
        if i != 0 or j != 0:
            part = piece(f, i, j)
            pltpu.make_async_copy(part, part, link_recv.at[f, i + 1, j + 3]).wait()
        x_first = FLOWS[f][0]
        if x_first or i == 0:
            for hop in children(Y_TREE, j):
                push(f, i, j, False, hop)
        if not x_first or j == 0:
            for hop in children(X_TREE, i):
                push(f, i, j, True, hop)
        share(f, i, j)

    def wave(level, t):
        for i in range(-1, NX - 1):
            for j in range(-3, NY - 3):
                if abs(i) + abs(j) == t:
                    for f in range(4 * level, 4 * level + 4):
                        visit(f, i, j)

    for s in range(1, NZ):
        pltpu.make_async_remote_copy(
            coef,
            probes.at[z],
            z_send,
            z_recv,
            device_id={"probe": lax.rem(z + s, NZ)},
            device_id_type=MESH,
        ).start()
    stage = (stage0, stage1)
    begun = 0

    def start_compute():
        for copy in local:
            copy.wait()
        share_bytes(chip_recv.at[0], 1 - core, 0)
        owner_slot = core * CHIPS + chip
        lists = [list_part(coarse_table, n, leaf) for n in range(2)]
        row, turn = slot_rows(lists[1], codes[FINE:], COARSE, 8, 0, owner_slot)
        coarse_staged[0:COARSE] = row
        coarse_staged[COARSE:] = turn
        move = pltpu.make_async_copy(coarse_staged, picks, own_sem.at[5])
        move.start()
        row, turn = slot_rows(lists[0], codes[0:FINE], FINE, 16, 1, owner_slot)
        staged[0:FINE] = row
        staged[FINE:] = turn
        move.wait()
        gather_all(coarse_table, picks, COARSE, 0, stage0)

    def body(n, carry):
        order = [n * CHUNK + u for u in range(CHUNK)]
        order.append(jnp.minimum((n + 1) * CHUNK, COARSE - 1))
        targets = []
        for u in range(CHUNK // 2):
            targets += feats_of(target_feats, FT + n * (CHUNK // 2) + u)
        outs = run_targets(coarse_table, picks, COARSE, order, targets, stage)
        for u in range(CHUNK):
            coarse_out[n * CHUNK + u] = jnp.concatenate(
                [outs[u], jnp.zeros((8, RANK), F32)], axis=1
            )
        return carry

    for kind, count in SCHEDULE:
        if kind != COMPUTE:
            wave(kind, count)
            continue
        if begun == 0:
            start_compute()
        lax.fori_loop(begun, begun + count, body, 0)
        begun += count

    own_coef.wait()
    share_bytes(chip_recv.at[1], 1 - core, 1)
    for level in range(2):
        share_bytes(chip_send.at[level], core, level)
        sent = tables[level].at[0 : (CHIPS - 1) * SIZES[level]]
        pltpu.make_async_copy(sent, sent, link_send.at[level]).wait()
    others = probes.at[0 : NZ - 1]
    pltpu.make_async_copy(others, others, z_recv).wait()
    pltpu.make_async_copy(others, others, z_send).wait()


def spread(coarse_payload, fine_payload, coef, feats, codes):
    dma = pltpu.SemaphoreType.DMA
    vm = pl.BlockSpec(memory_space=pltpu.VMEM)
    return pl.pallas_call(
        spread_kernel,
        out_shape=(
            jax.ShapeDtypeStruct((ENDS[1] + PAD, 16, 128), BF16),
            jax.ShapeDtypeStruct((NZ,) + coef.shape, BF16),
            jax.ShapeDtypeStruct((2 * FINE, 128), jnp.int32),
            jax.ShapeDtypeStruct((COARSE, 8, 128), F32),
        ),
        in_specs=[vm] * 5,
        out_specs=[vm] * 4,
        scratch_shapes=[
            pltpu.VMEM((ENDS[0] + PAD, 16, 128), BF16),
            pltpu.VMEM((2 * COARSE, 128), jnp.int32),
            pltpu.VMEM((PAD, 16, 128), BF16),
            pltpu.VMEM((PAIRS // 2, 16, 128), BF16),
            pltpu.VMEM((PAIRS // 2, 16, 128), BF16),
            pltpu.SMEM((2 * COARSE, 128), jnp.int32),
            dma((8, NX, NY)),
            dma((2,)),
            dma((2,)),
            dma((2,)),
            dma(()),
            dma(()),
            dma((6,)),
        ],
        compiler_params=pltpu.CompilerParams(
            collective_id=0, has_side_effects=True, vmem_limit_bytes=SPREAD_LIMIT
        ),
        name="spread",
    )(coarse_payload, fine_payload, coef, feats, codes)


def sweep_kernel(
    staged, tiles, target_feats, probes, transfer, coarse, far, partial, stage0, stage1, picks, sem
):
    z = lax.axis_index("probe")
    move = pltpu.make_async_copy(staged, picks, sem)
    move.start()
    move.wait()
    stage = (stage0, stage1)
    gather_all(tiles, picks, FINE, 0, stage0)

    def step(n, carry):
        order = [n * EACH + u for u in range(EACH)]
        order.append(jnp.minimum((n + 1) * EACH, FINE - 1))
        targets = []
        for u in range(EACH // 2):
            targets += feats_of(target_feats, n * (EACH // 2) + u)
        outs = run_targets(tiles, picks, FINE, order, targets, stage)
        for u in range(EACH // 2):
            q = n * (EACH // 2) + u
            cut = pl.ds(pl.multiple_of(q * 128, 128), 128)
            mats = transfer[:, cut]
            up = coarse[q]
            spread_up = jnp.concatenate([up, pltpu.roll(up, RANK, 1)], axis=0).astype(BF16)
            down = lax.dot_general(spread_up, mats, NT, preferred_element_type=F32)
            low, high = outs[2 * u : 2 * u + 2]
            far[:, cut] = jnp.concatenate([low + down[0:8], high + down[8:16]], axis=1)
        return carry

    lax.fori_loop(0, FINE // EACH, step, 0)

    whole = far[...]
    first = whole.astype(BF16)
    rest = whole - first.astype(F32)
    second = rest.astype(BF16)
    third = (rest - second.astype(F32)).astype(BF16)
    coefs = probes[...].reshape(NZ * 8, FINE * RANK)
    gram = (
        lax.dot_general(coefs, first, NT, preferred_element_type=F32)
        + lax.dot_general(coefs, second, NT, preferred_element_type=F32)
        + lax.dot_general(coefs, third, NT, preferred_element_type=F32)
    )
    wide = jnp.concatenate([gram, jnp.zeros((NZ * 8, 120), F32)], axis=1)
    partial[...] = pltpu.roll(wide, z * 8, 1)


def sweep(staged, table, feats, probes, transfer, coarse):
    vm = pl.BlockSpec(memory_space=pltpu.VMEM)
    return pl.pallas_call(
        sweep_kernel,
        out_shape=(
            jax.ShapeDtypeStruct((8, FINE * RANK), F32),
            jax.ShapeDtypeStruct((NZ * 8, 128), F32),
        ),
        in_specs=[vm] * 6,
        out_specs=[vm, vm],
        scratch_shapes=[
            pltpu.VMEM((PAIRS // 2, 16, 128), BF16),
            pltpu.VMEM((PAIRS // 2, 16, 128), BF16),
            pltpu.SMEM((2 * FINE, 128), jnp.int32),
            pltpu.SemaphoreType.DMA(()),
        ],
        compiler_params=pltpu.CompilerParams(vmem_limit_bytes=SWEEP_LIMIT),
        name="sweep",
    )(staged, table, feats, probes, transfer, coarse)


def reduce_kernel(gram_scale, partial, out, at_z, at_x, at_y, work, recv, send):
    leaf = lax.axis_index("leaf")
    z = lax.axis_index("probe")
    inner = lax.rem(leaf, 2 * NX)
    y = leaf // (2 * NX)

    def z_peer(s):
        return {"probe": lax.rem(z + s, NZ)}

    def x_peer(s):
        return {"leaf": y * (2 * NX) + lax.rem(inner + s, 2 * NX)}

    def y_peer(s):
        return {"leaf": lax.rem(y + s, NY) * (2 * NX) + inner}

    barrier = pltpu.get_barrier_semaphore()
    for peer in (z_peer, x_peer, y_peer):
        for s in range(1, 8):
            pl.semaphore_signal(barrier, 1, device_id=peer(s), device_id_type=MESH)
    pl.semaphore_wait(barrier, 21)

    def exchange(stage, peer, me, source, buffer):
        for s in range(1, 8):
            pltpu.make_async_remote_copy(
                source(s),
                buffer.at[me],
                send.at[stage],
                recv.at[stage],
                device_id=peer(s),
                device_id_type=MESH,
            ).start()
        buffer[me] = source(0)[...]
        got = buffer.at[0:7]
        pltpu.make_async_copy(got, got, recv.at[stage]).wait()
        total = buffer[0]
        for n in range(1, 8):
            total = total + buffer[n]
        pltpu.make_async_copy(got, got, send.at[stage]).wait()
        return total

    work[0] = exchange(0, z_peer, z, lambda s: partial.at[lax.rem(z + s, NZ)], at_z)
    work[1] = exchange(1, x_peer, inner, lambda s: work.at[0], at_x)
    out[...] = exchange(2, y_peer, y, lambda s: work.at[1], at_y) * gram_scale


def reduce_gram(partial, gram_scale):
    vm = pl.BlockSpec(memory_space=pltpu.VMEM)
    return pl.pallas_call(
        functools.partial(reduce_kernel, gram_scale),
        out_shape=jax.ShapeDtypeStruct((8, 128), F32),
        in_specs=[vm],
        out_specs=vm,
        scratch_shapes=[
            pltpu.VMEM((8, 8, 128), F32),
            pltpu.VMEM((8, 8, 128), F32),
            pltpu.VMEM((8, 8, 128), F32),
            pltpu.VMEM((2, 8, 128), F32),
            pltpu.SemaphoreType.DMA((3,)),
            pltpu.SemaphoreType.DMA((3,)),
        ],
        compiler_params=pltpu.CompilerParams(
            collective_id=1, has_side_effects=True, vmem_limit_bytes=1024 * 1024
        ),
        name="reduce_gram",
    )(partial)


def shards(
    coef_fine,
    points_fine,
    points_coarse,
    transfer,
    send_fine,
    slots_fine,
    counts_fine,
    send_coarse,
    slots_coarse,
    counts_coarse,
):
    arrays = (
        coef_fine,
        points_fine,
        points_coarse,
        transfer,
        send_fine[0].T,
        send_coarse[0].T,
        slots_fine,
        slots_coarse,
        counts_fine.reshape(1, FINE),
        counts_coarse.reshape(1, COARSE),
    )
    coarse_payload, fine_payload, feats, codes, coef, mats = prep(
        *[pltpu.with_memory_space_constraint(array, pltpu.HBM) for array in arrays]
    )
    table, probes, staged, coarse = spread(coarse_payload, fine_payload, coef, feats, codes)
    far, partial = sweep(staged, table, feats, probes, mats, coarse)
    gram_scale = 1.0 / math.sqrt(2 * CHIPS * FINE * RANK)
    gram = reduce_gram(partial.reshape(NZ, 8, 128), gram_scale)
    return (far, gram[:, 0 : NZ * 8])


def solution(mesh):
    return jax.shard_map(
        shards,
        mesh=mesh,
        in_specs=(
            P("probe", "leaf"),
            P(None, "leaf"),
            P(None, "leaf"),
            P(None, "leaf"),
            P("leaf", None, None),
            P("leaf", None),
            P("leaf"),
            P("leaf", None, None),
            P("leaf", None),
            P("leaf"),
        ),
        out_specs=(P("probe", "leaf"), P("probe", None)),
        check_vma=False,
    )
```
